512 devices in a mesh: xy: 32 (over x, z), gz: 16 (over y, core).
Axes of the slice: x: 4, y: 8, z: 8, core: 2. Of those that a mesh axis runs over, the one named last changes fastest.
Arguments:
- raw_tiles: bfloat16 [32, 32, 512, 512], P('gz', 'xy'), may hold values from -6 to 6
- src_tile: int32 [32, 1024, 1], P('gz'), may hold values from 0 to 31; in each aligned block of 32 rows (0 to 31, 32 to 63, ..., all dimensions but the last counted through in order) at most 2 rows name the same one
- shift_y: int32 [32, 1024], P('gz'), may hold values from 0 to 479
- shift_x: int32 [32, 1024], P('gz'), may hold values from 0 to 479
- subpixel: int32 [32, 1024], P('gz'), may hold values from 0 to 15
- owner_map: int32 [32], replicated, may hold values from 0 to 31, each once
- weight_one: bfloat16 [8, 1, 3, 3, 3], replicated, may hold values from -1.25 to 1.25
- bias_one: float32 [8], replicated, may hold values from -3 to 3
- weight_two: bfloat16 [8, 8, 3, 3, 3], replicated, may hold values from -0.4375 to 0.4375
- bias_two: float32 [8], replicated, may hold values from -3 to 3
Outputs:
- features: bfloat16 [8, 32, 2048, 512], P(None, 'gz', 'xy')
The draws below stay inside these ranges and needn't reach their ends.
Inputs may be any that keep to these rules, and one draw needn't show every extreme that they name: `src_tile`: within the 32 subtiles of one device's strip of one section (aligned blocks), no source tile is named more than 2 times; some source tile is named exactly 2 times in some block. `owner_map`: A permutation; slot p is stored on the device of index p // 1 along xy.
All inputs are finite; a program needn't handle non-finite values.
Results may differ from the reference program's by a relative error of at most 0.0054.
Values may be sent and summed in bfloat16 or wider, within the bound.
No kernel may reach another device: no remote copies, remote signals or barrier semaphores. Data moves between devices by JAX's collectives and lax.ppermute only.
A program may use at most 64 MiB of HBM per device.

```python
import math
import jax
import jax.numpy as jnp
import numpy as np
from jax import lax

CH = 8
SUB = 32
SGY = 2
SGX = 16
SS = 512
SUBS_DEV = 32
W = 512
NSEC = 32
NROWS = 2048
NSUB = 1024
SRCS = 32
CAP = 2
N_XY = 32


def place_ends(values, stream_key, low, largest):
    longest = values.shape.index(max(values.shape))
    spots = []
    for shift in (0, 1):
        where = [jax.random.randint(jax.random.fold_in(stream_key, axis), (), 0, length) for axis, length in enumerate(values.shape)]
        where[longest] = (where[longest] + shift) % values.shape[longest]
        spots.append(tuple(where))
    return values.at[spots[0]].set(low).at[spots[1]].set(largest)


def level_of(stream_key, shape, split, least, largest):
    factor_of, own = 1.0, jax.random.fold_in(stream_key, 6)
    for dim, blocks in split:
        draws = jnp.exp(jax.random.uniform(jax.random.fold_in(own, dim), (blocks,), jnp.float32, least / len(split), largest / len(split)))
        factor_of = factor_of * jnp.repeat(draws, shape[dim] // blocks).reshape([-1 if axis == dim else 1 for axis in range(len(shape))])
    return factor_of


def assign_block(rng, own, number, rows, number_of, top, reach, slope):
    sequence = jax.random.permutation(rng, number_of)
    packed, common = load_shares(number_of, rows * top, reach, slope, True), load_shares(number_of, rows * top, reach, slope, False)
    places = jnp.arange(number_of)

    def named(sizes, offset_by):
        used = int((sizes > 0).sum())
        fixed = max(1, used // 4)
        passed = fixed + (places - fixed + offset_by * (used - fixed)) % max(1, number_of - fixed)
        return jnp.zeros((number_of,), jnp.int32).at[sequence[jnp.where(places < fixed, places, passed)]].set(jnp.asarray(sizes, jnp.int32))

    sizes = jnp.where(number % 4 == 0, named(packed, number // 4), named(common, number - number // 4 - 1))
    mixed = jax.random.permutation(jax.random.fold_in(own, 3), number_of)
    source_of, receiver = mixed[0:number_of // 2 * 2:2], mixed[1:number_of // 2 * 2:2]
    room = jnp.minimum(sizes[source_of] - 1, reach - sizes[receiver]) // 2
    room = jnp.where((source_of == sequence[0]) | (receiver == sequence[0]) | (sizes[receiver] == 0), 0, jnp.maximum(room, 0))
    passed = jax.random.randint(jax.random.fold_in(own, 4), (number_of // 2,), 0, 1 << 20) % (room + 1)
    sizes = sizes.at[source_of].add(-passed).at[receiver].add(passed)
    members = jnp.searchsorted(jnp.cumsum(sizes), jnp.arange(rows * top), side="right").astype(jnp.int32)
    table = members.reshape(top, rows).T
    table = table[jax.random.permutation(jax.random.fold_in(own, 1), rows)]
    offset_by = jax.random.randint(jax.random.fold_in(own, 2), (rows, 1), 0, top)
    return jnp.take_along_axis(table, (jnp.arange(top)[None, :] + offset_by) % top, axis=1)


def load_shares(amount, total, bound, skew, full):
    weights = [(1 << 20) // math.isqrt(grade ** skew) + 1 for grade in range(1, amount + 1)]
    largest = bound if full else min(bound, max(-(-total // amount), total * weights[0] // sum(weights)))
    least = 1 if total - largest >= amount - 1 else 0
    holding, spare = [largest] + [least] * (amount - 1), total - largest - least * (amount - 1)
    while spare > 0:
        movable = [i for i in range(1, amount) if holding[i] < largest] or [i for i in range(1, amount) if holding[i] < bound]
        pool, left = sum([weights[i] for i in movable]), spare
        for i in movable:
            extra = min(bound - holding[i], max(1, left * weights[i] // pool), spare)
            holding[i] = holding[i] + extra
            spare = spare - extra
    return np.array(holding)


def gaussian(key, shape, width, most, shards=(), kind=jnp.bfloat16):
    loudness = level_of(key, shape, shards, -0.22, 0.18) if shards else 1.0
    values = jax.random.normal(key, shape, jnp.float32) * width * loudness
    return jnp.minimum(jnp.maximum(values, -most), most).astype(kind)


def setup_inputs(seed: int = 0) -> dict:
    keys = jax.random.split(jax.random.key(seed), 11)
    raw_tiles = gaussian(keys[0], (NSEC, SRCS, SS, SS), 1.0, 6.0, ((0, 16), (1, 32)))
    src_tile_keys = jax.random.split(jax.random.fold_in(keys[1], 1), NSEC * NSUB // SUBS_DEV)
    src_tile_turns = jax.random.permutation(jax.random.fold_in(keys[1], 3), NSEC * NSUB // SUBS_DEV)
    src_tile = jax.vmap(lambda own, number: assign_block(jax.random.fold_in(keys[1], 2), own, number, SUBS_DEV, SRCS, 1, CAP, 2))(src_tile_keys, src_tile_turns).reshape((NSEC, NSUB, 1))
    shift_y = place_ends(jax.random.randint(keys[2], (NSEC, NSUB), 0, SS - SUB), jax.random.fold_in(keys[2], 1), 0, (SS - SUB) - 1).astype(jnp.int32)
    shift_x = place_ends(jax.random.randint(keys[3], (NSEC, NSUB), 0, SS - SUB), jax.random.fold_in(keys[3], 1), 0, (SS - SUB) - 1).astype(jnp.int32)
    subpixel = place_ends(jax.random.randint(keys[4], (NSEC, NSUB), 0, 16), jax.random.fold_in(keys[4], 1), 0, 15).astype(jnp.int32)
    owner_map = jax.random.permutation(keys[5], SRCS).astype(jnp.int32)
    weight_one = gaussian(keys[6], (CH, 1, 3, 3, 3), 27 ** -0.5, 1.25)
    bias_one = gaussian(keys[7], (CH,), 0.5, 3.0, (), jnp.float32)
    weight_two = gaussian(keys[8], (CH, CH, 3, 3, 3), (27 * CH) ** -0.5, 0.4375)
    bias_two = gaussian(keys[9], (CH,), 0.5, 3.0, (), jnp.float32)
    return dict(raw_tiles=raw_tiles, src_tile=src_tile, shift_y=shift_y, shift_x=shift_x, subpixel=subpixel, owner_map=owner_map, weight_one=weight_one, bias_one=bias_one, weight_two=weight_two, bias_two=bias_two)


def convolve_layer(volume, weight, bias, rectify):
    padded = jnp.pad(volume, ((0, 0), (1, 1), (1, 1), (1, 1)))

    def one_section(z):
        slab = lax.dynamic_slice_in_dim(padded, z, 3, axis=1)
        result = lax.conv_general_dilated(slab[None], weight, (1, 1, 1), "VALID", dimension_numbers=("NCDHW", "OIDHW", "NCDHW"), preferred_element_type=jnp.float32)[0, :, 0]
        result = result + bias[:, None, None]
        if rectify:
            result = jax.nn.relu(result)
        return result.astype(jnp.bfloat16)

    stacked = lax.map(one_section, jnp.arange(NSEC, dtype=jnp.int32))
    return jnp.transpose(stacked, (1, 0, 2, 3))


def reference(raw_tiles, src_tile, shift_y, shift_x, subpixel, owner_map, weight_one, bias_one, weight_two, bias_two):
    source = jnp.take(raw_tiles, owner_map, axis=1)
    tile_ids = src_tile[:, :, 0].reshape(-1).astype(jnp.int32)
    section_ids = jnp.broadcast_to(jnp.arange(NSEC, dtype=jnp.int32)[:, None], (NSEC, NSUB)).reshape(-1)
    tops = shift_y.reshape(-1).astype(jnp.int32)
    lefts = shift_x.reshape(-1).astype(jnp.int32)

    def window(z, k, y, x):
        return lax.dynamic_slice(source, (z, k, y, x), (1, 1, SUB + 1, SUB + 1))[0, 0]

    patches = jax.vmap(window)(section_ids, tile_ids, tops, lefts).astype(jnp.float32)
    codes = subpixel.reshape(-1)
    frac_y = ((codes // 4).astype(jnp.float32) / 4.0)[:, None, None]
    frac_x = ((codes % 4).astype(jnp.float32) / 4.0)[:, None, None]
    rendered = ((1.0 - frac_y) * (1.0 - frac_x) * patches[:, :-1, :-1] + (1.0 - frac_y) * frac_x * patches[:, :-1, 1:]
                + frac_y * (1.0 - frac_x) * patches[:, 1:, :-1] + frac_y * frac_x * patches[:, 1:, 1:])
    rendered = rendered.astype(jnp.bfloat16)
    image = rendered.reshape(NSEC, N_XY, SGY, SGX, SUB, SUB)
    image = jnp.transpose(image, (0, 1, 2, 4, 3, 5)).reshape(NSEC, NROWS, W)
    hidden = convolve_layer(image[None], weight_one, bias_one, True)
    return convolve_layer(hidden, weight_two, bias_two, False)
```

```python
import jax
import jax.numpy as jnp
from jax import lax
from jax.experimental import pallas as pl
from jax.experimental.pallas import tpu as pltpu
from jax.sharding import PartitionSpec as P

SUB = 32
W = 512
HID_ROWS = 22
WIN_ROWS = 24
IMG_ROWS = 80
F32 = jnp.float32
BF16 = jnp.bfloat16


def iota(shape, dim):
    return lax.broadcasted_iota(jnp.int32, shape, dim)


def by_index(which, choices):
    result = choices[-1]
    for number in range(len(choices) - 2, -1, -1):
        result = jnp.where(which == number, choices[number], result)
    return result


def render_kernel(table, tiles, out, wide):
    parts = out.shape[0]
    sections = tiles.shape[0]
    for z in range(sections):
        for t in range(4):
            wide[z, t] = tiles[z, :, 128 * t : 128 * t + 128].astype(F32)
    lane = iota((8, 128), 1)
    group = lane // 32
    lane_tall = iota((SUB, 128), 1)

    def one(q, z, slot):
        code = table[(z * parts + q) * 2 + slot]
        y = code & 511
        x = (code >> 9) & 511
        a = ((code >> 20) & 3).astype(F32) * 0.25
        b = ((code >> 18) & 3).astype(F32) * 0.25
        near = x >> 7
        far = jnp.minimum(near + 1, 3)
        low = x & 127
        wraps = lane_tall < low
        upper = jnp.where(wraps, wide[z, far, pl.ds(y, SUB), :], wide[z, near, pl.ds(y, SUB), :])
        lower = jnp.where(
            wraps, wide[z, far, pl.ds(y + 1, SUB), :], wide[z, near, pl.ds(y + 1, SUB), :]
        )
        mixed = (1.0 - a) * upper + a * lower
        here, right = [], []
        for g in range(4):
            piece = mixed[8 * g : 8 * g + 8]
            here.append(pltpu.roll(piece, (32 * g + 128 - low) & 127, 1))
            right.append(pltpu.roll(piece, (32 * g + 127 - low) & 127, 1))
        value = (1.0 - b) * by_index(group, here) + b * by_index(group, right)
        out[q, z * 2 + slot] = value.astype(BF16)

    @pl.loop(0, parts)
    def _(q):
        for z in range(sections):
            for slot in range(2):
                one(q, z, slot)

    sub = iota((8, 128), 0)
    which = jnp.where(sub < 4, group, (group + 1) & 3)

    @pl.loop(0, parts)
    def _(q):
        after = jnp.minimum(q + 1, parts - 1)
        before = jnp.maximum(q - 1, 0)
        turned = []
        for zs in range(4):
            both = jnp.where(sub < 4, out[after, zs].astype(F32), out[before, zs].astype(F32))
            turned.append(both if zs == 0 else pltpu.roll(both, 32 * zs, 1))
        out[q, 4] = by_index(which, turned).astype(BF16)


def assemble_kernel(table, flags, pool, image):
    lane = iota((8, 128), 1)
    group = lane // 32
    sections = image.shape[0]

    def entry(z, strip, s):
        packed = table[(z * 3 + strip) * 32 + s]
        return packed >> 1, 2 * z + (packed & 1)

    for z in range(sections):
        for c in range(4):
            rows = []
            heads, feet = [], []
            for v in range(4):
                k, zs = entry(z, 0, 16 + 4 * c + v)
                piece = pool[k, 4].astype(F32)
                heads.append(pltpu.roll(piece, (32 * (v - zs - 3) + 256) & 127, 1))
                k, zs = entry(z, 2, 4 * c + v)
                piece = pool[k, 4].astype(F32)
                feet.append(pltpu.roll(piece, (32 * (v - zs) + 256) & 127, 1))
            rows.append(jnp.where(flags[0] == 0, 0.0, by_index(group, heads)))
            for u in range(2):
                blocks = []
                for v in range(4):
                    k, zs = entry(z, 1, 16 * u + 4 * c + v)
                    blocks.append(pool[k, zs].astype(F32))
                for g in range(4):
                    turned = [
                        blocks[v] if v == g else pltpu.roll(blocks[v], (32 * (v - g)) % 128, 1)
                        for v in range(4)
                    ]
                    rows.append(by_index(group, turned))
            rows.append(jnp.where(flags[1] == 0, 0.0, by_index(group, feet)))
            image[z, :, 128 * c : 128 * c + 128] = jnp.concatenate(rows, axis=0).astype(BF16)


def band_kernel(flat_one, flat_two, one, two):
    rows, cols = one.shape
    col = iota((27, cols), 1)
    base = (col // WIN_ROWS) % 3 * 9 + col // (3 * WIN_ROWS)
    offset = iota((rows, cols), 1) % WIN_ROWS - iota((rows, cols), 0) // 8
    total = jnp.zeros((rows, cols), F32)
    for e in range(3):
        picks = (iota((27, cols), 0) == base + 3 * e).astype(F32).astype(BF16)
        taps = jnp.dot(flat_one[...], picks, preferred_element_type=F32)
        total = jnp.where(offset == e, jnp.concatenate([taps] * (rows // 8), axis=0), total)
    one[...] = total.astype(BF16)

    rows, cols = two.shape
    col = iota((216, cols), 1)
    base = col % 8 * 27 + col // 80 * 9
    spread = (iota((rows, 24), 0) // 8 == iota((rows, 24), 1)).astype(F32).astype(BF16)
    offset = iota((rows, cols), 1) % 80 // 8 - iota((rows, cols), 0) % 8
    total = jnp.zeros((rows, cols), F32)
    for e in range(3):
        parts = []
        for f in range(3):
            picks = (iota((216, cols), 0) == base + (3 * e + f)).astype(F32).astype(BF16)
            parts.append(jnp.dot(flat_two[...], picks, preferred_element_type=F32))
        taps = jnp.concatenate(parts, axis=0).astype(BF16)
        total = jnp.where(offset == e, jnp.dot(spread, taps, preferred_element_type=F32), total)
    two[...] = total.astype(BF16)


def conv_kernel(flags, bias_two, bias_one, before, own, after, one, two, out, shifted, hidden):
    lane = iota((IMG_ROWS, W), 1)
    for number, (ref, z) in enumerate(
        [(before, 0), (before, 1), (own, 0), (own, 1), (after, 0), (after, 1)]
    ):
        plane = ref[z].astype(F32)
        shifted[number, 0] = jnp.where(lane == 0, 0.0, pltpu.roll(plane, 1, 1))
        shifted[number, 1] = plane
        shifted[number, 2] = jnp.where(lane == W - 1, 0.0, pltpu.roll(plane, W - 1, 1))
    gain = bias_one[...][:, :1]
    height = HID_ROWS * 8
    row = iota((height, W), 0)
    for p in range(4):
        for b in range(3):
            start = HID_ROWS * b + 6
            stack = jnp.concatenate(
                [
                    shifted[p + d, f, start : start + WIN_ROWS, :]
                    for f in range(3)
                    for d in range(3)
                ],
                axis=0,
            ).astype(BF16)
            total = jnp.dot(one[...], stack, preferred_element_type=F32)
            total = jnp.maximum(total.reshape(HID_ROWS, 8, W) + gain, 0.0).reshape(height, W)
            if b == 0:
                total = jnp.where(jnp.logical_or(row >= 8, flags[0] != 0), total, 0.0)
            if b == 2:
                total = jnp.where(jnp.logical_or(row < height - 8, flags[1] != 0), total, 0.0)
            hidden[p, height * b : height * b + height, :] = total.astype(BF16)

    @pl.when(flags[2] == 0)
    def _():
        hidden[0] = jnp.zeros(hidden.shape[1:], BF16)

    @pl.when(flags[3] == 0)
    def _():
        hidden[3] = jnp.zeros(hidden.shape[1:], BF16)

    edge = iota((64, W), 1)
    for z in range(2):
        for pair in range(4):
            halves = []
            for b in (2 * pair, 2 * pair + 1):
                stack = jnp.concatenate(
                    [hidden[z + d, 64 * b : 64 * b + 80, :] for d in range(3)], axis=0
                )
                total = jnp.dot(two[...], stack, preferred_element_type=F32)
                left = jnp.where(edge == 0, 0.0, pltpu.roll(total[0:64], 1, 1))
                right = jnp.where(edge == W - 1, 0.0, pltpu.roll(total[128:192], W - 1, 1))
                halves.append(total[64:128] + left + right)
            for o in range(8):
                both = jnp.concatenate([half[8 * o : 8 * o + 8] for half in halves], axis=0)
                out[o, z, 16 * pair : 16 * pair + 16, :] = (both + bias_two[o]).astype(BF16)


def smem():
    return pl.BlockSpec(memory_space=pltpu.SMEM)


def vmem():
    return pl.BlockSpec(memory_space=pltpu.VMEM)


def on_device(
    raw_tiles,
    src_tile,
    shift_y,
    shift_x,
    subpixel,
    owner_map,
    weight_one,
    bias_one,
    weight_two,
    bias_two,
):
    parts = lax.axis_size("xy")
    depth = lax.axis_size("gz")
    me = lax.axis_index("xy")
    deep = lax.axis_index("gz")
    sections = raw_tiles.shape[0]
    source = src_tile.reshape(sections, parts, 32)
    packed = (shift_y + (shift_x << 9) + (subpixel << 18)).reshape(sections, parts, 32)
    tile_ids = jnp.arange(parts, dtype=jnp.int32)
    mine = jnp.sum(jnp.where(owner_map == me, tile_ids, 0))
    number = jnp.arange(32, dtype=jnp.int32)
    match = source == mine
    first = jnp.min(jnp.where(match, number, 31), axis=-1)
    last = jnp.max(jnp.where(match, number, 0), axis=-1)
    chosen = jnp.stack([first, last], axis=-1)
    table = jnp.sum(
        jnp.where(chosen[..., None] == number, packed[:, :, None, :], 0), axis=-1
    ).reshape(-1)

    outgoing = pl.pallas_call(
        render_kernel,
        out_shape=jax.ShapeDtypeStruct((parts, 5, 8, 128), BF16),
        in_specs=[smem(), vmem()],
        out_specs=vmem(),
        scratch_shapes=[pltpu.VMEM((sections, 4, 512, 128), F32)],
        name="render",
    )(table, raw_tiles.reshape(sections, 512, 512))

    received = lax.all_to_all(outgoing, "xy", split_axis=0, concat_axis=0, tiled=True)

    around = jnp.clip(me + jnp.arange(-1, 2, dtype=jnp.int32), 0, parts - 1)
    near = jnp.sum(
        jnp.where(
            around[None, :, None, None] == tile_ids[None, None, :, None], source[:, None], 0
        ),
        axis=2,
    )
    holder = jnp.sum(jnp.where(near[..., None] == tile_ids, owner_map, 0), axis=-1)
    second = jnp.any(
        jnp.logical_and(
            near[..., :, None] == near[..., None, :], number[None, :] < number[:, None]
        ),
        axis=-1,
    )
    places = (holder * 2 + second.astype(jnp.int32)).reshape(-1)
    flags = jnp.stack([me > 0, me < parts - 1, deep > 0, deep < depth - 1]).astype(jnp.int32)

    image = pl.pallas_call(
        assemble_kernel,
        out_shape=jax.ShapeDtypeStruct((sections, IMG_ROWS, W), BF16),
        in_specs=[smem(), smem(), vmem()],
        out_specs=vmem(),
        name="assemble",
    )(places, flags, received)

    before = lax.ppermute(image, "gz", [(i, i + 1) for i in range(depth - 1)])
    after = lax.ppermute(image, "gz", [(i + 1, i) for i in range(depth - 1)])

    banded_one, banded_two = pl.pallas_call(
        band_kernel,
        out_shape=(
            jax.ShapeDtypeStruct((HID_ROWS * 8, 9 * WIN_ROWS), BF16),
            jax.ShapeDtypeStruct((192, 240), BF16),
        ),
        in_specs=[vmem(), vmem()],
        out_specs=(vmem(), vmem()),
        name="bands",
    )(weight_one.reshape(8, 27), weight_two.reshape(8, 216))

    return pl.pallas_call(
        conv_kernel,
        out_shape=jax.ShapeDtypeStruct((8, sections, 64, W), BF16),
        in_specs=[smem(), smem()] + [vmem()] * 6,
        out_specs=vmem(),
        scratch_shapes=[
            pltpu.VMEM((6, 3, IMG_ROWS, W), F32),
            pltpu.VMEM((4, 66 * 8, W), BF16),
        ],
        name="convolve",
    )(
        flags,
        bias_two,
        jnp.broadcast_to(bias_one[:, None], (8, 128)),
        before,
        image,
        after,
        banded_one,
        banded_two,
    )


def solution(mesh):
    in_specs = (
        P("gz", "xy", None, None),
        P("gz", None, None),
        P("gz", None),
        P("gz", None),
        P("gz", None),
        P(),
        P(),
        P(),
        P(),
        P(),
    )
    out_specs = P(None, "gz", "xy", None)
    return jax.shard_map(
        on_device, mesh=mesh, in_specs=in_specs, out_specs=out_specs, check_vma=False
    )
```

```python
import jax
import jax.numpy as jnp
from jax import lax
from jax.experimental import pallas as pl
from jax.experimental.pallas import tpu as pltpu
from jax.sharding import PartitionSpec as P

SUB = 32
W = 512
HID_ROWS = 22
WIN_ROWS = 24
IMG_ROWS = 80
MAIN_UNROLL = 8
HALO_UNROLL = 8
F32 = jnp.float32
BF16 = jnp.bfloat16


def iota(shape, dim):
    return lax.broadcasted_iota(jnp.int32, shape, dim)


def by_index(which, choices):
    result = choices[-1]
    for number in range(len(choices) - 2, -1, -1):
        result = jnp.where(which == number, choices[number], result)
    return result


def render_kernel(
    owner, source, tops, lefts, codes, tiles, out, landing, wide, found, table, arrived, listed
):
    parts = out.shape[0]
    sections = tiles.shape[0]
    copies = [
        pltpu.make_async_copy(tiles.at[z], landing.at[z], arrived.at[z]) for z in range(sections)
    ]
    for copy in copies:
        copy.start()

    me = lax.axis_index("xy")
    mine = jnp.int32(0)
    for k in range(parts):
        mine = jnp.where(owner[k] == me, k, mine)
    count = source.shape[2]
    blank = jnp.full((8 - sections, count), -1, jnp.int32)
    match = jnp.concatenate([source[z] for z in range(sections)] + [blank], axis=0) == mine
    within = iota((8, count), 1) & 31
    rank = match.astype(jnp.int32)
    for reach in (1, 2, 4, 8, 16):
        rank = rank + jnp.where(within >= reach, pltpu.roll(rank, reach, 1), 0)
    packed = tops[...] + (lefts[...] << 9) + (codes[...] << 18)
    packed = jnp.concatenate([packed, blank], axis=0)
    pieces = []
    for slot in range(2):
        chosen = jnp.where(jnp.logical_and(match, rank == slot + 1), packed, 0)
        for k in range(3):
            pieces.append(((chosen >> (8 * k)) & 255).astype(F32))
    strips = (iota((count, 128), 0) // 32 == iota((count, 128), 1)).astype(F32).astype(BF16)
    sums = jnp.dot(
        jnp.concatenate(pieces, axis=0).astype(BF16), strips, preferred_element_type=F32
    ).astype(jnp.int32)
    pair = [
        sums[24 * slot : 24 * slot + 8]
        + (sums[24 * slot + 8 : 24 * slot + 16] << 8)
        + (sums[24 * slot + 16 : 24 * slot + 24] << 16)
        for slot in range(2)
    ]
    found[...] = jnp.where(iota((8, 128), 0) < 2, pair[0], pltpu.roll(pair[1], 2, 0))
    listing = pltpu.make_async_copy(found, table, listed.at[0])
    listing.start()

    for z in range(sections):
        copies[z].wait()
        for t in range(4):
            wide[z, t] = landing[z, :, 128 * t : 128 * t + 128].astype(F32)
    listing.wait()
    lane = iota((8, 128), 1)
    group = lane // 32
    lane_tall = iota((SUB, 128), 1)

    def one(q, z, slot):
        code = table[2 * slot + z, q]
        y = code & 511
        x = (code >> 9) & 511
        a = ((code >> 20) & 3).astype(F32) * 0.25
        b = ((code >> 18) & 3).astype(F32) * 0.25
        near = x >> 7
        far = jnp.minimum(near + 1, 3)
        low = x & 127
        wraps = lane_tall < low
        upper = jnp.where(wraps, wide[z, far, pl.ds(y, SUB), :], wide[z, near, pl.ds(y, SUB), :])
        lower = jnp.where(
            wraps, wide[z, far, pl.ds(y + 1, SUB), :], wide[z, near, pl.ds(y + 1, SUB), :]
        )
        mixed = (1.0 - a) * upper + a * lower
        here, right = [], []
        for g in range(4):
            piece = mixed[8 * g : 8 * g + 8]
            here.append(pltpu.roll(piece, (32 * g + 128 - low) & 127, 1))
            right.append(pltpu.roll(piece, (32 * g + 127 - low) & 127, 1))
        value = (1.0 - b) * by_index(group, here) + b * by_index(group, right)
        out[q, z * 2 + slot] = value.astype(BF16)

    @pl.loop(0, parts, unroll=MAIN_UNROLL)
    def _(q):
        for z in range(sections):
            for slot in range(2):
                one(q, z, slot)

    sub = iota((8, 128), 0)
    which = jnp.where(sub < 4, group, (group + 1) & 3)

    @pl.loop(0, parts, unroll=HALO_UNROLL)
    def _(q):
        after = jnp.minimum(q + 1, parts - 1)
        before = jnp.maximum(q - 1, 0)
        turned = []
        for zs in range(4):
            both = jnp.where(sub < 4, out[after, zs].astype(F32), out[before, zs].astype(F32))
            turned.append(both if zs == 0 else pltpu.roll(both, 32 * zs, 1))
        out[q, 4] = by_index(which, turned).astype(BF16)


def assemble_kernel(table, flags, pool, image):
    lane = iota((8, 128), 1)
    group = lane // 32
    sections = image.shape[0]

    def entry(z, strip, s):
        packed = table[(z * 3 + strip) * 32 + s]
        return packed >> 1, 2 * z + (packed & 1)

    for z in range(sections):
        for c in range(4):
            rows = []
            heads, feet = [], []
            for v in range(4):
                k, zs = entry(z, 0, 16 + 4 * c + v)
                piece = pool[k, 4].astype(F32)
                heads.append(pltpu.roll(piece, (32 * (v - zs - 3) + 256) & 127, 1))
                k, zs = entry(z, 2, 4 * c + v)
                piece = pool[k, 4].astype(F32)
                feet.append(pltpu.roll(piece, (32 * (v - zs) + 256) & 127, 1))
            rows.append(jnp.where(flags[0] == 0, 0.0, by_index(group, heads)))
            for u in range(2):
                blocks = []
                for v in range(4):
                    k, zs = entry(z, 1, 16 * u + 4 * c + v)
                    blocks.append(pool[k, zs].astype(F32))
                for g in range(4):
                    turned = [
                        blocks[v] if v == g else pltpu.roll(blocks[v], (32 * (v - g)) % 128, 1)
                        for v in range(4)
                    ]
                    rows.append(by_index(group, turned))
            rows.append(jnp.where(flags[1] == 0, 0.0, by_index(group, feet)))
            image[z, :, 128 * c : 128 * c + 128] = jnp.concatenate(rows, axis=0).astype(BF16)


def band_kernel(flat_one, flat_two, one, two):
    rows, cols = one.shape
    col = iota((27, cols), 1)
    base = (col // WIN_ROWS) % 3 * 9 + col // (3 * WIN_ROWS)
    offset = iota((rows, cols), 1) % WIN_ROWS - iota((rows, cols), 0) // 8
    total = jnp.zeros((rows, cols), F32)
    for e in range(3):
        picks = (iota((27, cols), 0) == base + 3 * e).astype(F32).astype(BF16)
        taps = jnp.dot(flat_one[...], picks, preferred_element_type=F32)
        total = jnp.where(offset == e, jnp.concatenate([taps] * (rows // 8), axis=0), total)
    one[...] = total.astype(BF16)

    rows, cols = two.shape
    col = iota((216, cols), 1)
    base = col % 8 * 27 + col // 80 * 9
    spread = (iota((rows, 24), 0) // 8 == iota((rows, 24), 1)).astype(F32).astype(BF16)
    offset = iota((rows, cols), 1) % 80 // 8 - iota((rows, cols), 0) % 8
    total = jnp.zeros((rows, cols), F32)
    for e in range(3):
        parts = []
        for f in range(3):
            picks = (iota((216, cols), 0) == base + (3 * e + f)).astype(F32).astype(BF16)
            parts.append(jnp.dot(flat_two[...], picks, preferred_element_type=F32))
        taps = jnp.concatenate(parts, axis=0).astype(BF16)
        total = jnp.where(offset == e, jnp.dot(spread, taps, preferred_element_type=F32), total)
    two[...] = total.astype(BF16)


def conv_kernel(flags, bias_one, bias_two, before, own, after, one, two, out, shifted, hidden):
    lane = iota((IMG_ROWS, W), 1)
    for number, (ref, z) in enumerate(
        [(before, 0), (before, 1), (own, 0), (own, 1), (after, 0), (after, 1)]
    ):
        plane = ref[z].astype(F32)
        if number < 2:
            plane = jnp.where(flags[2] == 0, 0.0, plane)
        if number >= 4:
            plane = jnp.where(flags[3] == 0, 0.0, plane)
        shifted[number, 0] = jnp.where(lane == 0, 0.0, pltpu.roll(plane, 1, 1))
        shifted[number, 1] = plane
        shifted[number, 2] = jnp.where(lane == W - 1, 0.0, pltpu.roll(plane, W - 1, 1))
    row = iota((8, W), 0)
    gain = by_index(row, [bias_one[o] for o in range(8)])
    height = HID_ROWS * 8
    row = iota((height, W), 0)
    for p in range(4):
        for b in range(3):
            start = HID_ROWS * b + 6
            stack = jnp.concatenate(
                [
                    shifted[p + d, f, start : start + WIN_ROWS, :]
                    for f in range(3)
                    for d in range(3)
                ],
                axis=0,
            ).astype(BF16)
            total = jnp.dot(one[...], stack, preferred_element_type=F32)
            total = jnp.maximum(total.reshape(HID_ROWS, 8, W) + gain, 0.0).reshape(height, W)
            if b == 0:
                total = jnp.where(jnp.logical_or(row >= 8, flags[0] != 0), total, 0.0)
            if b == 2:
                total = jnp.where(jnp.logical_or(row < height - 8, flags[1] != 0), total, 0.0)
            hidden[p, height * b : height * b + height, :] = total.astype(BF16)

    @pl.when(flags[2] == 0)
    def _():
        hidden[0] = jnp.zeros(hidden.shape[1:], BF16)

    @pl.when(flags[3] == 0)
    def _():
        hidden[3] = jnp.zeros(hidden.shape[1:], BF16)

    edge = iota((64, W), 1)
    for z in range(2):
        for pair in range(4):
            halves = []
            for b in (2 * pair, 2 * pair + 1):
                stack = jnp.concatenate(
                    [hidden[z + d, 64 * b : 64 * b + 80, :] for d in range(3)], axis=0
                )
                total = jnp.dot(two[...], stack, preferred_element_type=F32)
                left = jnp.where(edge == 0, 0.0, pltpu.roll(total[0:64], 1, 1))
                right = jnp.where(edge == W - 1, 0.0, pltpu.roll(total[128:192], W - 1, 1))
                halves.append(total[64:128] + left + right)
            for o in range(8):
                both = jnp.concatenate([half[8 * o : 8 * o + 8] for half in halves], axis=0)
                out[o, z, 16 * pair : 16 * pair + 16, :] = (both + bias_two[o]).astype(BF16)


def smem():
    return pl.BlockSpec(memory_space=pltpu.SMEM)


def vmem():
    return pl.BlockSpec(memory_space=pltpu.VMEM)


def on_device(
    raw_tiles,
    src_tile,
    shift_y,
    shift_x,
    subpixel,
    owner_map,
    weight_one,
    bias_one,
    weight_two,
    bias_two,
):
    parts = lax.axis_size("xy")
    depth = lax.axis_size("gz")
    me = lax.axis_index("xy")
    deep = lax.axis_index("gz")
    sections = raw_tiles.shape[0]
    source = src_tile.reshape(sections, parts, 32)
    tile_ids = jnp.arange(parts, dtype=jnp.int32)
    number = jnp.arange(32, dtype=jnp.int32)

    outgoing = pl.pallas_call(
        render_kernel,
        out_shape=jax.ShapeDtypeStruct((parts, 5, 8, 128), BF16),
        in_specs=[smem()] + [vmem()] * 4 + [pl.BlockSpec(memory_space=pl.ANY)],
        out_specs=vmem(),
        scratch_shapes=[
            pltpu.VMEM((sections, 512, 512), BF16),
            pltpu.VMEM((sections, 4, 512, 128), F32),
            pltpu.VMEM((8, 128), jnp.int32),
            pltpu.SMEM((8, 128), jnp.int32),
            pltpu.SemaphoreType.DMA((sections,)),
            pltpu.SemaphoreType.DMA((1,)),
        ],
        name="render",
    )(
        owner_map,
        src_tile.reshape(sections, 1, parts * 32),
        shift_y,
        shift_x,
        subpixel,
        raw_tiles.reshape(sections, 512, 512),
    )

    received = lax.all_to_all(outgoing, "xy", split_axis=0, concat_axis=0, tiled=True)

    around = jnp.clip(me + jnp.arange(-1, 2, dtype=jnp.int32), 0, parts - 1)
    near = jnp.sum(
        jnp.where(
            around[None, :, None, None] == tile_ids[None, None, :, None], source[:, None], 0
        ),
        axis=2,
    )
    holder = jnp.sum(jnp.where(near[..., None] == tile_ids, owner_map, 0), axis=-1)
    second = jnp.any(
        jnp.logical_and(
            near[..., :, None] == near[..., None, :], number[None, :] < number[:, None]
        ),
        axis=-1,
    )
    places = (holder * 2 + second.astype(jnp.int32)).reshape(-1)
    flags = jnp.stack([me > 0, me < parts - 1, deep > 0, deep < depth - 1]).astype(jnp.int32)

    banded_one, banded_two = pl.pallas_call(
        band_kernel,
        out_shape=(
            jax.ShapeDtypeStruct((HID_ROWS * 8, 9 * WIN_ROWS), BF16),
            jax.ShapeDtypeStruct((192, 240), BF16),
        ),
        in_specs=[vmem(), vmem()],
        out_specs=(vmem(), vmem()),
        name="bands",
    )(weight_one.reshape(8, 27), weight_two.reshape(8, 216))

    received, places, flags, banded_one, banded_two = lax.optimization_barrier(
        (received, places, flags, banded_one, banded_two)
    )
    image = pl.pallas_call(
        assemble_kernel,
        out_shape=jax.ShapeDtypeStruct((sections, IMG_ROWS, W), BF16),
        in_specs=[smem(), smem(), vmem()],
        out_specs=vmem(),
        name="assemble",
    )(places, flags, received)

    before = lax.ppermute(image, "gz", [(i, (i + 1) % depth) for i in range(depth)])
    after = lax.ppermute(image, "gz", [((i + 1) % depth, i) for i in range(depth)])

    return pl.pallas_call(
        conv_kernel,
        out_shape=jax.ShapeDtypeStruct((8, sections, 64, W), BF16),
        in_specs=[smem()] * 3 + [vmem()] * 5,
        out_specs=vmem(),
        scratch_shapes=[
            pltpu.VMEM((6, 3, IMG_ROWS, W), F32),
            pltpu.VMEM((4, 66 * 8, W), BF16),
        ],
        name="convolve",
    )(
        flags,
        bias_one,
        bias_two,
        before,
        image,
        after,
        banded_one,
        banded_two,
    )


def solution(mesh):
    in_specs = (
        P("gz", "xy", None, None),
        P("gz", None, None),
        P("gz", None),
        P("gz", None),
        P("gz", None),
        P(),
        P(),
        P(),
        P(),
        P(),
    )
    out_specs = P(None, "gz", "xy", None)
    return jax.shard_map(
        on_device, mesh=mesh, in_specs=in_specs, out_specs=out_specs, check_vma=False
    )
```

```python
import jax
import jax.numpy as jnp
from jax import lax
from jax.experimental import pallas as pl
from jax.experimental.pallas import tpu as pltpu
from jax.sharding import PartitionSpec as P

SUB = 32
W = 512
HID_ROWS = 22
WIN_ROWS = 24
IMG_ROWS = 80
MAIN_UNROLL = 8
HALO_UNROLL = 8
F32 = jnp.float32
BF16 = jnp.bfloat16


def iota(shape, dim):
    return lax.broadcasted_iota(jnp.int32, shape, dim)


def by_index(which, choices):
    result = choices[-1]
    for number in range(len(choices) - 2, -1, -1):
        result = jnp.where(which == number, choices[number], result)
    return result


def render_kernel(
    owner, source, tops, lefts, codes, tiles, out, landing, wide, found, table, arrived, listed
):
    parts = out.shape[0]
    sections = tiles.shape[0]
    copies = [
        pltpu.make_async_copy(tiles.at[z], landing.at[z], arrived.at[z]) for z in range(sections)
    ]
    for copy in copies:
        copy.start()

    me = lax.axis_index("xy")
    mine = jnp.int32(0)
    for k in range(parts):
        mine = jnp.where(owner[k] == me, k, mine)
    count = source.shape[2]
    blank = jnp.full((8 - sections, count), -1, jnp.int32)
    match = jnp.concatenate([source[z] for z in range(sections)] + [blank], axis=0) == mine
    within = iota((8, count), 1) & 31
    rank = match.astype(jnp.int32)
    for reach in (1, 2, 4, 8, 16):
        rank = rank + jnp.where(within >= reach, pltpu.roll(rank, reach, 1), 0)
    packed = tops[...] + (lefts[...] << 9) + (codes[...] << 18)
    packed = jnp.concatenate([packed, blank], axis=0)
    pieces = []
    for slot in range(2):
        chosen = jnp.where(jnp.logical_and(match, rank == slot + 1), packed, 0)
        for k in range(3):
            pieces.append(((chosen >> (8 * k)) & 255).astype(F32))
    strips = (iota((count, 128), 0) // 32 == iota((count, 128), 1)).astype(F32).astype(BF16)
    sums = jnp.dot(
        jnp.concatenate(pieces, axis=0).astype(BF16), strips, preferred_element_type=F32
    ).astype(jnp.int32)
    pair = [
        sums[24 * slot : 24 * slot + 8]
        + (sums[24 * slot + 8 : 24 * slot + 16] << 8)
        + (sums[24 * slot + 16 : 24 * slot + 24] << 16)
        for slot in range(2)
    ]
    found[...] = jnp.where(iota((8, 128), 0) < 2, pair[0], pltpu.roll(pair[1], 2, 0))
    listing = pltpu.make_async_copy(found, table, listed.at[0])
    listing.start()

    for z in range(sections):
        copies[z].wait()
        for t in range(4):
            wide[z, t] = landing[z, :, 128 * t : 128 * t + 128].astype(F32)
    listing.wait()
    lane = iota((8, 128), 1)
    group = lane // 32
    lane_tall = iota((SUB, 128), 1)

    def one(q, z, slot):
        code = table[2 * slot + z, q]
        y = code & 511
        x = (code >> 9) & 511
        a = ((code >> 20) & 3).astype(F32) * 0.25
        b = ((code >> 18) & 3).astype(F32) * 0.25
        near = x >> 7
        far = jnp.minimum(near + 1, 3)
        low = x & 127
        wraps = lane_tall < low
        upper = jnp.where(wraps, wide[z, far, pl.ds(y, SUB), :], wide[z, near, pl.ds(y, SUB), :])
        lower = jnp.where(
            wraps, wide[z, far, pl.ds(y + 1, SUB), :], wide[z, near, pl.ds(y + 1, SUB), :]
        )
        mixed = (1.0 - a) * upper + a * lower
        here, right = [], []
        for g in range(4):
            piece = mixed[8 * g : 8 * g + 8]
            here.append(pltpu.roll(piece, (32 * g + 128 - low) & 127, 1))
            right.append(pltpu.roll(piece, (32 * g + 127 - low) & 127, 1))
        value = (1.0 - b) * by_index(group, here) + b * by_index(group, right)
        out[q, z * 2 + slot] = value.astype(BF16)

    @pl.loop(0, parts, unroll=MAIN_UNROLL)
    def _(q):
        for z in range(sections):
            for slot in range(2):
                one(q, z, slot)

    sub = iota((8, 128), 0)
    which = jnp.where(sub < 4, group, (group + 1) & 3)

    @pl.loop(0, parts, unroll=HALO_UNROLL)
    def _(q):
        after = jnp.minimum(q + 1, parts - 1)
        before = jnp.maximum(q - 1, 0)
        turned = []
        for zs in range(4):
            both = jnp.where(sub < 4, out[after, zs].astype(F32), out[before, zs].astype(F32))
            turned.append(both if zs == 0 else pltpu.roll(both, 32 * zs, 1))
        out[q, 4] = by_index(which, turned).astype(BF16)


def assemble_kernel(table, flags, pool, image):
    lane = iota((8, 128), 1)
    group = lane // 32
    sections = image.shape[0]

    def entry(z, strip, s):
        packed = table[(z * 3 + strip) * 32 + s]
        return packed >> 1, 2 * z + (packed & 1)

    for z in range(sections):
        for c in range(4):
            rows = []
            heads, feet = [], []
            for v in range(4):
                k, zs = entry(z, 0, 16 + 4 * c + v)
                piece = pool[k, 4].astype(F32)
                heads.append(pltpu.roll(piece, (32 * (v - zs - 3) + 256) & 127, 1))
                k, zs = entry(z, 2, 4 * c + v)
                piece = pool[k, 4].astype(F32)
                feet.append(pltpu.roll(piece, (32 * (v - zs) + 256) & 127, 1))
            rows.append(jnp.where(flags[0] == 0, 0.0, by_index(group, heads)))
            for u in range(2):
                blocks = []
                for v in range(4):
                    k, zs = entry(z, 1, 16 * u + 4 * c + v)
                    blocks.append(pool[k, zs].astype(F32))
                for g in range(4):
                    turned = [
                        blocks[v] if v == g else pltpu.roll(blocks[v], (32 * (v - g)) % 128, 1)
                        for v in range(4)
                    ]
                    rows.append(by_index(group, turned))
            rows.append(jnp.where(flags[1] == 0, 0.0, by_index(group, feet)))
            image[z, :, 128 * c : 128 * c + 128] = jnp.concatenate(rows, axis=0).astype(BF16)


def band_kernel(flat_one, flat_two, one, two):
    rows, cols = one.shape
    col = iota((27, cols), 1)
    base = (col // WIN_ROWS) % 3 * 9 + col // (3 * WIN_ROWS)
    offset = iota((rows, cols), 1) % WIN_ROWS - iota((rows, cols), 0) // 8
    total = jnp.zeros((rows, cols), F32)
    for e in range(3):
        picks = (iota((27, cols), 0) == base + 3 * e).astype(F32).astype(BF16)
        taps = jnp.dot(flat_one[...], picks, preferred_element_type=F32)
        total = jnp.where(offset == e, jnp.concatenate([taps] * (rows // 8), axis=0), total)
    one[...] = total.astype(BF16)

    rows, cols = two.shape
    col = iota((216, cols), 1)
    base = col % 8 * 27 + col // 80 * 9
    spread = (iota((rows, 24), 0) // 8 == iota((rows, 24), 1)).astype(F32).astype(BF16)
    offset = iota((rows, cols), 1) % 80 // 8 - iota((rows, cols), 0) % 8
    total = jnp.zeros((rows, cols), F32)
    for e in range(3):
        parts = []
        for f in range(3):
            picks = (iota((216, cols), 0) == base + (3 * e + f)).astype(F32).astype(BF16)
            parts.append(jnp.dot(flat_two[...], picks, preferred_element_type=F32))
        taps = jnp.concatenate(parts, axis=0).astype(BF16)
        total = jnp.where(offset == e, jnp.dot(spread, taps, preferred_element_type=F32), total)
    two[...] = total.astype(BF16)


def conv_kernel(
    flags, bias_one, bias_two, before, own, after, one, two, out, shifted, hidden, stage, sent
):
    lane = iota((IMG_ROWS, W), 1)
    for number, (ref, z) in enumerate(
        [(before, 0), (before, 1), (own, 0), (own, 1), (after, 0), (after, 1)]
    ):
        plane = ref[z].astype(F32)
        if number < 2:
            plane = jnp.where(flags[2] == 0, 0.0, plane)
        if number >= 4:
            plane = jnp.where(flags[3] == 0, 0.0, plane)
        shifted[number, 0] = jnp.where(lane == 0, 0.0, pltpu.roll(plane, 1, 1))
        shifted[number, 1] = plane
        shifted[number, 2] = jnp.where(lane == W - 1, 0.0, pltpu.roll(plane, W - 1, 1))
    row = iota((8, W), 0)
    gain = by_index(row, [bias_one[o] for o in range(8)])
    height = HID_ROWS * 8
    row = iota((height, W), 0)
    for p in range(4):
        for b in range(3):
            start = HID_ROWS * b + 6
            stack = jnp.concatenate(
                [
                    shifted[p + d, f, start : start + WIN_ROWS, :]
                    for f in range(3)
                    for d in range(3)
                ],
                axis=0,
            ).astype(BF16)
            total = jnp.dot(one[...], stack, preferred_element_type=F32)
            total = jnp.maximum(total.reshape(HID_ROWS, 8, W) + gain, 0.0).reshape(height, W)
            if b == 0:
                total = jnp.where(jnp.logical_or(row >= 8, flags[0] != 0), total, 0.0)
            if b == 2:
                total = jnp.where(jnp.logical_or(row < height - 8, flags[1] != 0), total, 0.0)
            hidden[p, height * b : height * b + height, :] = total.astype(BF16)

    @pl.when(flags[2] == 0)
    def _():
        hidden[0] = jnp.zeros(hidden.shape[1:], BF16)

    @pl.when(flags[3] == 0)
    def _():
        hidden[3] = jnp.zeros(hidden.shape[1:], BF16)

    edge = iota((64, W), 1)
    copies = []
    for z in range(2):
        for pair in range(4):
            halves = []
            for b in (2 * pair, 2 * pair + 1):
                stack = jnp.concatenate(
                    [hidden[z + d, 64 * b : 64 * b + 80, :] for d in range(3)], axis=0
                )
                total = jnp.dot(two[...], stack, preferred_element_type=F32)
                left = jnp.where(edge == 0, 0.0, pltpu.roll(total[0:64], 1, 1))
                right = jnp.where(edge == W - 1, 0.0, pltpu.roll(total[128:192], W - 1, 1))
                halves.append(total[64:128] + left + right)
            rows = pl.ds(16 * pair, 16)
            for o in range(8):
                both = jnp.concatenate([half[8 * o : 8 * o + 8] for half in halves], axis=0)
                stage[o, z, rows, :] = (both + bias_two[o]).astype(BF16)
            copy = pltpu.make_async_copy(
                stage.at[:, z, rows, :], out.at[:, z, rows, :], sent.at[4 * z + pair]
            )
            copy.start()
            copies.append(copy)
    for copy in copies:
        copy.wait()


def smem():
    return pl.BlockSpec(memory_space=pltpu.SMEM)


def vmem():
    return pl.BlockSpec(memory_space=pltpu.VMEM)


def in_vmem(array):
    return pltpu.with_memory_space_constraint(array, pltpu.VMEM)


def in_smem(array):
    return pltpu.with_memory_space_constraint(array, pltpu.SMEM)


def on_device(
    raw_tiles,
    src_tile,
    shift_y,
    shift_x,
    subpixel,
    owner_map,
    weight_one,
    bias_one,
    weight_two,
    bias_two,
):
    parts = lax.axis_size("xy")
    depth = lax.axis_size("gz")
    me = lax.axis_index("xy")
    deep = lax.axis_index("gz")
    sections = raw_tiles.shape[0]
    source = src_tile.reshape(sections, parts, 32)
    tile_ids = jnp.arange(parts, dtype=jnp.int32)
    number = jnp.arange(32, dtype=jnp.int32)

    outgoing = pl.pallas_call(
        render_kernel,
        out_shape=pltpu.VMEM((parts, 5, 8, 128), BF16),
        in_specs=[smem()] + [vmem()] * 4 + [pl.BlockSpec(memory_space=pl.ANY)],
        out_specs=vmem(),
        scratch_shapes=[
            pltpu.VMEM((sections, 512, 512), BF16),
            pltpu.VMEM((sections, 4, 512, 128), F32),
            pltpu.VMEM((8, 128), jnp.int32),
            pltpu.SMEM((8, 128), jnp.int32),
            pltpu.SemaphoreType.DMA((sections,)),
            pltpu.SemaphoreType.DMA((1,)),
        ],
        name="render",
    )(
        owner_map,
        src_tile.reshape(sections, 1, parts * 32),
        shift_y,
        shift_x,
        subpixel,
        raw_tiles.reshape(sections, 512, 512),
    )

    received = lax.all_to_all(outgoing, "xy", split_axis=0, concat_axis=0, tiled=True)

    around = jnp.clip(me + jnp.arange(-1, 2, dtype=jnp.int32), 0, parts - 1)
    near = jnp.sum(
        jnp.where(
            around[None, :, None, None] == tile_ids[None, None, :, None], source[:, None], 0
        ),
        axis=2,
    )
    holder = jnp.sum(jnp.where(near[..., None] == tile_ids, owner_map, 0), axis=-1)
    second = jnp.any(
        jnp.logical_and(
            near[..., :, None] == near[..., None, :], number[None, :] < number[:, None]
        ),
        axis=-1,
    )
    places = (holder * 2 + second.astype(jnp.int32)).reshape(-1)
    flags = jnp.stack([me > 0, me < parts - 1, deep > 0, deep < depth - 1]).astype(jnp.int32)

    banded_one, banded_two = pl.pallas_call(
        band_kernel,
        out_shape=(
            pltpu.VMEM((HID_ROWS * 8, 9 * WIN_ROWS), BF16),
            pltpu.VMEM((192, 240), BF16),
        ),
        in_specs=[vmem(), vmem()],
        out_specs=(vmem(), vmem()),
        name="bands",
    )(weight_one.reshape(8, 27), weight_two.reshape(8, 216))

    received, places, flags, banded_one, banded_two = lax.optimization_barrier(
        (received, places, flags, banded_one, banded_two)
    )
    image = pl.pallas_call(
        assemble_kernel,
        out_shape=pltpu.VMEM((sections, IMG_ROWS, W), BF16),
        in_specs=[smem(), smem(), vmem()],
        out_specs=vmem(),
        name="assemble",
    )(in_smem(places), in_smem(flags), in_vmem(received))

    before = lax.ppermute(image, "gz", [(i, (i + 1) % depth) for i in range(depth)])
    after = lax.ppermute(image, "gz", [((i + 1) % depth, i) for i in range(depth)])

    return pl.pallas_call(
        conv_kernel,
        out_shape=jax.ShapeDtypeStruct((8, sections, 64, W), BF16),
        in_specs=[smem()] * 3 + [vmem()] * 5,
        out_specs=pl.BlockSpec(memory_space=pl.ANY),
        scratch_shapes=[
            pltpu.VMEM((6, 3, IMG_ROWS, W), F32),
            pltpu.VMEM((4, 66 * 8, W), BF16),
            pltpu.VMEM((8, sections, 64, W), BF16),
            pltpu.SemaphoreType.DMA((4 * sections,)),
        ],
        name="convolve",
    )(
        in_smem(flags),
        bias_one,
        bias_two,
        in_vmem(before),
        in_vmem(image),
        in_vmem(after),
        in_vmem(banded_one),
        in_vmem(banded_two),
    )


def solution(mesh):
    in_specs = (
        P("gz", "xy", None, None),
        P("gz", None, None),
        P("gz", None),
        P("gz", None),
        P("gz", None),
        P(),
        P(),
        P(),
        P(),
        P(),
    )
    out_specs = P(None, "gz", "xy", None)
    return jax.shard_map(
        on_device, mesh=mesh, in_specs=in_specs, out_specs=out_specs, check_vma=False
    )
```

```python
import jax
import jax.numpy as jnp
from jax import lax
from jax.experimental import pallas as pl
from jax.experimental.pallas import tpu as pltpu
from jax.sharding import PartitionSpec as P

SUB = 32
W = 512
HID_ROWS = 22
WIN_ROWS = 24
IMG_ROWS = 80
BATCH = 8
MAIN_UNROLL = 8
HALO_UNROLL = 4
UNROLL_ONE = 4
UNROLL_TWO = 8
F32 = jnp.float32
BF16 = jnp.bfloat16


def iota(shape, dim):
    return lax.broadcasted_iota(jnp.int32, shape, dim)


def by_index(which, choices):
    result = choices[-1]
    for number in range(len(choices) - 2, -1, -1):
        result = jnp.where(which == number, choices[number], result)
    return result


def render_kernel(
    owner_in,
    source_in,
    tops_in,
    lefts_in,
    codes_in,
    tiles,
    out,
    owner,
    source,
    tops,
    lefts,
    codes,
    landing,
    wide,
    kept,
    ready,
    found,
    table,
    arrived,
    landed,
    listed,
    sent,
):
    parts = out.shape[0]
    sections = tiles.shape[0]
    small = [
        pltpu.make_async_copy(src, dst, arrived.at[n])
        for n, (src, dst) in enumerate(
            [
                (source_in, source),
                (owner_in, owner),
                (tops_in, tops),
                (lefts_in, lefts),
                (codes_in, codes),
            ]
        )
    ]
    half = landing.shape[1] // 2
    copies = [
        pltpu.make_async_copy(
            tiles.at[z, pl.ds(half * h, half), :],
            landing.at[z, pl.ds(half * h, half), :],
            landed.at[2 * z + h],
        )
        for z in range(sections)
        for h in range(2)
    ]
    for copy in small + copies:
        copy.start()
    for copy in small:
        copy.wait()

    me = lax.axis_index("xy")
    mine = jnp.int32(0)
    for k in range(parts):
        mine = jnp.where(owner[k] == me, k, mine)
    count = source.shape[2]
    blank = jnp.full((8 - sections, count), -1, jnp.int32)
    match = jnp.concatenate([source[z] for z in range(sections)] + [blank], axis=0) == mine
    within = iota((8, count), 1) & 31
    rank = match.astype(jnp.int32)
    for reach in (1, 2, 4, 8, 16):
        rank = rank + jnp.where(within >= reach, pltpu.roll(rank, reach, 1), 0)
    packed = tops[...] + (lefts[...] << 9) + (codes[...] << 18)
    packed = jnp.concatenate([packed, blank], axis=0)
    pieces = []
    for slot in range(2):
        chosen = jnp.where(jnp.logical_and(match, rank == slot + 1), packed, 0)
        for k in range(3):
            pieces.append(((chosen >> (8 * k)) & 255).astype(F32))
    strips = (iota((count, 128), 0) // 32 == iota((count, 128), 1)).astype(F32).astype(BF16)
    sums = jnp.dot(
        jnp.concatenate(pieces, axis=0).astype(BF16), strips, preferred_element_type=F32
    ).astype(jnp.int32)
    pair = [
        sums[24 * slot : 24 * slot + 8]
        + (sums[24 * slot + 8 : 24 * slot + 16] << 8)
        + (sums[24 * slot + 16 : 24 * slot + 24] << 16)
        for slot in range(2)
    ]
    found[...] = jnp.where(iota((8, 128), 0) < 2, pair[0], pltpu.roll(pair[1], 2, 0))
    listing = pltpu.make_async_copy(found, table, listed.at[0])
    listing.start()

    for z in range(sections):
        for h in range(2):
            copies[2 * z + h].wait()
            rows = pl.ds(half * h, half)
            for t in range(4):
                wide[z, t, rows, :] = landing[z, rows, 128 * t : 128 * t + 128].astype(F32)
    listing.wait()
    lane = iota((8, 128), 1)
    group = lane // 32
    starts = lane % 32 == 0

    def one(q, z, slot):
        code = table[2 * slot + z, q]
        y = code & 511
        x = (code >> 9) & 511
        a = ((code >> 20) & 3).astype(F32) * 0.25
        b = ((code >> 18) & 3).astype(F32) * 0.25
        near = x >> 7
        far = jnp.minimum(near + 1, 3)
        low = x & 127
        wraps = lane < low
        here = []
        for g in range(4):
            upper = jnp.where(
                wraps, wide[z, far, pl.ds(y + 8 * g, 8), :], wide[z, near, pl.ds(y + 8 * g, 8), :]
            )
            lower = jnp.where(
                wraps,
                wide[z, far, pl.ds(y + (8 * g + 1), 8), :],
                wide[z, near, pl.ds(y + (8 * g + 1), 8), :],
            )
            mixed = (1.0 - a) * upper + a * lower
            here.append(pltpu.roll(mixed, (32 * g + 128 - low) & 127, 1))
        left = by_index(group, here)
        spill = by_index(group, here[3:] + here[:3])
        right = pltpu.roll(jnp.where(starts, spill, left), 127, 1)
        value = (1.0 - b) * left + b * right
        zs = z * 2 + slot
        ready[q, zs] = value.astype(BF16)
        kept[q, zs] = value if zs == 0 else pltpu.roll(value, 32 * zs, 1)

    sub = iota((8, 128), 0)
    which = jnp.where(sub < 4, group, (group + 1) & 3)

    def finish(batch):
        @pl.loop(0, BATCH, unroll=HALO_UNROLL)
        def _(step):
            q = batch * BATCH + step
            after = jnp.minimum(q + 1, parts - 1)
            before = jnp.maximum(q - 1, 0)
            both = [
                jnp.where(sub < 4, kept[after, zs], kept[before, zs]) for zs in range(2 * sections)
            ]
            ready[q, 2 * sections] = by_index(which, both).astype(BF16)

        sending(batch).start()

    def sending(batch):
        strips = pl.ds(batch * BATCH, BATCH)
        return pltpu.make_async_copy(ready.at[strips], out.at[strips], sent.at[batch])

    batches = parts // BATCH

    @pl.loop(0, batches)
    def _(batch):
        @pl.loop(0, BATCH, unroll=MAIN_UNROLL)
        def _(step):
            for z in range(sections):
                for slot in range(2):
                    one(batch * BATCH + step, z, slot)

        @pl.when(batch > 0)
        def _():
            finish(batch - 1)

    finish(batches - 1)

    @pl.loop(0, batches)
    def _(batch):
        sending(batch).wait()


def assemble_kernel(table, flags, pool, image):
    lane = iota((8, 128), 1)
    group = lane // 32
    sections = image.shape[0]

    def entry(z, strip, s):
        packed = table[(z * 3 + strip) * 32 + s]
        return packed >> 1, 2 * z + (packed & 1)

    for z in range(sections):
        for c in range(4):
            rows = []
            heads, feet = [], []
            for v in range(4):
                k, zs = entry(z, 0, 16 + 4 * c + v)
                piece = pool[k, 4].astype(F32)
                heads.append(pltpu.roll(piece, (32 * (v - zs - 3) + 256) & 127, 1))
                k, zs = entry(z, 2, 4 * c + v)
                piece = pool[k, 4].astype(F32)
                feet.append(pltpu.roll(piece, (32 * (v - zs) + 256) & 127, 1))
            rows.append(jnp.where(flags[0] == 0, 0.0, by_index(group, heads)))
            for u in range(2):
                blocks = []
                for v in range(4):
                    k, zs = entry(z, 1, 16 * u + 4 * c + v)
                    blocks.append(pool[k, zs].astype(F32))
                for g in range(4):
                    turned = [
                        blocks[v] if v == g else pltpu.roll(blocks[v], (32 * (v - g)) % 128, 1)
                        for v in range(4)
                    ]
                    rows.append(by_index(group, turned))
            rows.append(jnp.where(flags[1] == 0, 0.0, by_index(group, feet)))
            image[z, :, 128 * c : 128 * c + 128] = jnp.concatenate(rows, axis=0).astype(BF16)


def band_kernel(flat_one, flat_two, one, two):
    rows, cols = one.shape
    col = iota((27, cols), 1)
    base = (col // WIN_ROWS) % 3 * 9 + col // (3 * WIN_ROWS)
    offset = iota((rows, cols), 1) % WIN_ROWS - iota((rows, cols), 0) // 8
    total = jnp.zeros((rows, cols), F32)
    for e in range(3):
        picks = (iota((27, cols), 0) == base + 3 * e).astype(F32).astype(BF16)
        taps = jnp.dot(flat_one[...], picks, preferred_element_type=F32)
        total = jnp.where(offset == e, jnp.concatenate([taps] * (rows // 8), axis=0), total)
    one[...] = total.astype(BF16)

    rows, cols = two.shape
    col = iota((216, cols), 1)
    base = col % 8 * 27 + col // 80 * 9
    spread = (iota((rows, 24), 0) // 8 == iota((rows, 24), 1)).astype(F32).astype(BF16)
    offset = iota((rows, cols), 1) % 80 // 8 - iota((rows, cols), 0) % 8
    total = jnp.zeros((rows, cols), F32)
    for e in range(3):
        parts = []
        for f in range(3):
            picks = (iota((216, cols), 0) == base + (3 * e + f)).astype(F32).astype(BF16)
            parts.append(jnp.dot(flat_two[...], picks, preferred_element_type=F32))
        taps = jnp.concatenate(parts, axis=0).astype(BF16)
        total = jnp.where(offset == e, jnp.dot(spread, taps, preferred_element_type=F32), total)
    two[...] = total.astype(BF16)


def conv_kernel(
    flags, bias_one, bias_two, before, own, after, one, two, out, shifted, hidden, stage, sent
):
    lane = iota((IMG_ROWS, W), 1)
    for number, (ref, z) in enumerate(
        [(before, 0), (before, 1), (own, 0), (own, 1), (after, 0), (after, 1)]
    ):
        plane = ref[z].astype(F32)
        if number < 2:
            plane = jnp.where(flags[2] == 0, 0.0, plane)
        if number >= 4:
            plane = jnp.where(flags[3] == 0, 0.0, plane)
        shifted[number, 0] = jnp.where(lane == 0, 0.0, pltpu.roll(plane, 1, 1))
        shifted[number, 1] = plane
        shifted[number, 2] = jnp.where(lane == W - 1, 0.0, pltpu.roll(plane, W - 1, 1))
    row = iota((8, W), 0)
    gain = by_index(row, [bias_one[o] for o in range(8)])
    height = HID_ROWS * 8

    @pl.loop(0, 4, unroll=UNROLL_ONE)
    def _(p):
        for b in range(3):
            start = HID_ROWS * b + 6
            stack = jnp.concatenate(
                [
                    shifted[p + d, f, start : start + WIN_ROWS, :]
                    for f in range(3)
                    for d in range(3)
                ],
                axis=0,
            ).astype(BF16)
            total = jnp.dot(one[...], stack, preferred_element_type=F32)
            total = jnp.maximum(total.reshape(HID_ROWS, 8, W) + gain, 0.0)
            keep = jnp.logical_and(
                jnp.logical_or(p > 0, flags[2] != 0), jnp.logical_or(p < 3, flags[3] != 0)
            )
            layers = [total[r] for r in range(HID_ROWS)]
            if b == 0:
                layers[0] = jnp.where(flags[0] != 0, layers[0], 0.0)
            if b == 2:
                layers[-1] = jnp.where(flags[1] != 0, layers[-1], 0.0)
            total = jnp.where(keep, jnp.concatenate(layers, axis=0), 0.0)
            hidden[p, height * b : height * b + height, :] = total.astype(BF16)

    edge = iota((64, W), 1)

    def sending(z, pair):
        rows = pl.ds(pl.multiple_of(16 * pair, 16), 16)
        return pltpu.make_async_copy(
            stage.at[:, z, rows, :], out.at[:, z, rows, :], sent.at[4 * z + pair]
        )

    @pl.loop(0, 8, unroll=UNROLL_TWO)
    def _(turn):
        z = turn >> 2
        pair = turn & 3
        halves = []
        for b in range(2):
            rows = pl.ds(pl.multiple_of(128 * pair + 64 * b, 64), 80)
            stack = jnp.concatenate([hidden[z + d, rows, :] for d in range(3)], axis=0)
            total = jnp.dot(two[...], stack, preferred_element_type=F32)
            left = jnp.where(edge == 0, 0.0, pltpu.roll(total[0:64], 1, 1))
            right = jnp.where(edge == W - 1, 0.0, pltpu.roll(total[128:192], W - 1, 1))
            halves.append(total[64:128] + left + right)
        rows = pl.ds(pl.multiple_of(16 * pair, 16), 16)
        for o in range(8):
            both = jnp.concatenate([half[8 * o : 8 * o + 8] for half in halves], axis=0)
            stage[o, z, rows, :] = (both + bias_two[o]).astype(BF16)
        sending(z, pair).start()

    @pl.loop(0, 8)
    def _(turn):
        sending(turn >> 2, turn & 3).wait()


def smem():
    return pl.BlockSpec(memory_space=pltpu.SMEM)


def vmem():
    return pl.BlockSpec(memory_space=pltpu.VMEM)


def in_vmem(array):
    return pltpu.with_memory_space_constraint(array, pltpu.VMEM)


def in_smem(array):
    return pltpu.with_memory_space_constraint(array, pltpu.SMEM)


def on_device(
    raw_tiles,
    src_tile,
    shift_y,
    shift_x,
    subpixel,
    owner_map,
    weight_one,
    bias_one,
    weight_two,
    bias_two,
):
    parts = lax.axis_size("xy")
    depth = lax.axis_size("gz")
    me = lax.axis_index("xy")
    deep = lax.axis_index("gz")
    sections = raw_tiles.shape[0]
    source = src_tile.reshape(sections, parts, 32)
    tile_ids = jnp.arange(parts, dtype=jnp.int32)
    number = jnp.arange(32, dtype=jnp.int32)

    outgoing = pl.pallas_call(
        render_kernel,
        out_shape=jax.ShapeDtypeStruct((parts, 5, 8, 128), BF16),
        in_specs=[pl.BlockSpec(memory_space=pl.ANY)] * 6,
        out_specs=pl.BlockSpec(memory_space=pl.ANY),
        scratch_shapes=[
            pltpu.SMEM((parts,), jnp.int32),
            pltpu.VMEM((sections, 1, parts * 32), jnp.int32),
            pltpu.VMEM((sections, parts * 32), jnp.int32),
            pltpu.VMEM((sections, parts * 32), jnp.int32),
            pltpu.VMEM((sections, parts * 32), jnp.int32),
            pltpu.VMEM((sections, 512, 512), BF16),
            pltpu.VMEM((sections, 4, 512, 128), F32),
            pltpu.VMEM((parts, 2 * sections, 8, 128), F32),
            pltpu.VMEM((parts, 5, 8, 128), BF16),
            pltpu.VMEM((8, 128), jnp.int32),
            pltpu.SMEM((8, 128), jnp.int32),
            pltpu.SemaphoreType.DMA((5,)),
            pltpu.SemaphoreType.DMA((2 * sections,)),
            pltpu.SemaphoreType.DMA((1,)),
            pltpu.SemaphoreType.DMA((parts // BATCH,)),
        ],
        name="render",
    )(
        owner_map,
        src_tile.reshape(sections, 1, parts * 32),
        shift_y,
        shift_x,
        subpixel,
        raw_tiles.reshape(sections, 512, 512),
    )

    received = lax.all_to_all(outgoing, "xy", split_axis=0, concat_axis=0, tiled=True)

    around = jnp.clip(me + jnp.arange(-1, 2, dtype=jnp.int32), 0, parts - 1)
    near = jnp.sum(
        jnp.where(
            around[None, :, None, None] == tile_ids[None, None, :, None], source[:, None], 0
        ),
        axis=2,
    )
    holder = jnp.sum(jnp.where(near[..., None] == tile_ids, owner_map, 0), axis=-1)
    second = jnp.any(
        jnp.logical_and(
            near[..., :, None] == near[..., None, :], number[None, :] < number[:, None]
        ),
        axis=-1,
    )
    places = (holder * 2 + second.astype(jnp.int32)).reshape(-1)
    flags = jnp.stack([me > 0, me < parts - 1, deep > 0, deep < depth - 1]).astype(jnp.int32)

    banded_one, banded_two = pl.pallas_call(
        band_kernel,
        out_shape=(
            pltpu.VMEM((HID_ROWS * 8, 9 * WIN_ROWS), BF16),
            pltpu.VMEM((192, 240), BF16),
        ),
        in_specs=[vmem(), vmem()],
        out_specs=(vmem(), vmem()),
        name="bands",
    )(weight_one.reshape(8, 27), weight_two.reshape(8, 216))

    received, places, flags, banded_one, banded_two = lax.optimization_barrier(
        (received, places, flags, banded_one, banded_two)
    )
    image = pl.pallas_call(
        assemble_kernel,
        out_shape=pltpu.VMEM((sections, IMG_ROWS, W), BF16),
        in_specs=[smem(), smem(), vmem()],
        out_specs=vmem(),
        name="assemble",
    )(in_smem(places), in_smem(flags), in_vmem(received))

    before = lax.ppermute(image, "gz", [(i, (i + 1) % depth) for i in range(depth)])
    after = lax.ppermute(image, "gz", [((i + 1) % depth, i) for i in range(depth)])

    return pl.pallas_call(
        conv_kernel,
        out_shape=jax.ShapeDtypeStruct((8, sections, 64, W), BF16),
        in_specs=[smem()] * 3 + [vmem()] * 5,
        out_specs=pl.BlockSpec(memory_space=pl.ANY),
        scratch_shapes=[
            pltpu.VMEM((6, 3, IMG_ROWS, W), F32),
            pltpu.VMEM((4, 66 * 8, W), BF16),
            pltpu.VMEM((8, sections, 64, W), BF16),
            pltpu.SemaphoreType.DMA((4 * sections,)),
        ],
        name="convolve",
    )(
        in_smem(flags),
        bias_one,
        bias_two,
        in_vmem(before),
        in_vmem(image),
        in_vmem(after),
        in_vmem(banded_one),
        in_vmem(banded_two),
    )


def solution(mesh):
    in_specs = (
        P("gz", "xy", None, None),
        P("gz", None, None),
        P("gz", None),
        P("gz", None),
        P("gz", None),
        P(),
        P(),
        P(),
        P(),
        P(),
    )
    out_specs = P(None, "gz", "xy", None)
    return jax.shard_map(
        on_device, mesh=mesh, in_specs=in_specs, out_specs=out_specs, check_vma=False
    )
```

```python
import jax
import jax.numpy as jnp
from jax import lax
from jax.experimental import pallas as pl
from jax.experimental.pallas import tpu as pltpu
from jax.sharding import PartitionSpec as P

SUB = 32
W = 512
HID_ROWS = 22
WIN_ROWS = 24
IMG_ROWS = 72
BATCH = 8
MAIN_UNROLL = 8
HALO_UNROLL = 4
UNROLL_ONE = 4
UNROLL_TWO = 8
F32 = jnp.float32
BF16 = jnp.bfloat16


def iota(shape, dim):
    return lax.broadcasted_iota(jnp.int32, shape, dim)


def by_index(which, choices):
    result = choices[-1]
    for number in range(len(choices) - 2, -1, -1):
        result = jnp.where(which == number, choices[number], result)
    return result


def render_kernel(
    owner_in,
    source_in,
    tops_in,
    lefts_in,
    codes_in,
    tiles,
    out,
    owner,
    source,
    tops,
    lefts,
    codes,
    landing,
    wide,
    kept,
    ready,
    found,
    table,
    arrived,
    landed,
    listed,
    sent,
):
    parts = out.shape[0]
    sections = tiles.shape[0]
    small = [
        pltpu.make_async_copy(src, dst, arrived.at[n])
        for n, (src, dst) in enumerate(
            [
                (source_in, source),
                (owner_in, owner),
                (tops_in, tops),
                (lefts_in, lefts),
                (codes_in, codes),
            ]
        )
    ]
    half = landing.shape[1] // 2
    copies = [
        pltpu.make_async_copy(
            tiles.at[z, pl.ds(half * h, half), :],
            landing.at[z, pl.ds(half * h, half), :],
            landed.at[2 * z + h],
        )
        for z in range(sections)
        for h in range(2)
    ]
    for copy in small + copies:
        copy.start()
    for copy in small:
        copy.wait()

    me = lax.axis_index("xy")
    mine = jnp.int32(0)
    for k in range(parts):
        mine = jnp.where(owner[k] == me, k, mine)
    count = source.shape[2]
    blank = jnp.full((8 - sections, count), -1, jnp.int32)
    match = jnp.concatenate([source[z] for z in range(sections)] + [blank], axis=0) == mine
    marks = match.astype(F32)
    tall = jnp.concatenate([marks[:, t : t + 128] for t in range(0, count, 128)], axis=0)
    early, late = iota((128, 128), 0), iota((128, 128), 1)
    upto = jnp.logical_and(early // 32 == late // 32, early <= late).astype(F32)
    ranks = jnp.dot(tall.astype(BF16), upto.astype(BF16), preferred_element_type=F32)
    rank = jnp.concatenate([ranks[t : t + 8] for t in range(0, count // 16, 8)], axis=1)
    packed = tops[...] + (lefts[...] << 9) + (codes[...] << 18)
    packed = jnp.concatenate([packed, blank], axis=0)
    pieces = []
    for slot in range(2):
        chosen = jnp.where(jnp.logical_and(match, rank == slot + 1), packed, 0)
        for k in range(3):
            pieces.append(((chosen >> (8 * k)) & 255).astype(F32))
    strips = (iota((count, 128), 0) // 32 == iota((count, 128), 1)).astype(F32).astype(BF16)
    sums = jnp.dot(
        jnp.concatenate(pieces, axis=0).astype(BF16), strips, preferred_element_type=F32
    ).astype(jnp.int32)
    pair = [
        sums[24 * slot : 24 * slot + 8]
        + (sums[24 * slot + 8 : 24 * slot + 16] << 8)
        + (sums[24 * slot + 16 : 24 * slot + 24] << 16)
        for slot in range(2)
    ]
    found[...] = jnp.where(iota((8, 128), 0) < 2, pair[0], pltpu.roll(pair[1], 2, 0))
    listing = pltpu.make_async_copy(found, table, listed.at[0])
    listing.start()

    for z in range(sections):
        for h in range(2):
            copies[2 * z + h].wait()
            rows = pl.ds(half * h, half)
            for t in range(4):
                wide[z, t, rows, :] = landing[z, rows, 128 * t : 128 * t + 128].astype(F32)
    listing.wait()
    lane = iota((8, 128), 1)
    group = lane // 32
    starts = lane % 32 == 0

    def one(q, z, slot):
        code = table[2 * slot + z, q]
        y = code & 511
        x = (code >> 9) & 511
        a = ((code >> 20) & 3).astype(F32) * 0.25
        b = ((code >> 18) & 3).astype(F32) * 0.25
        near = x >> 7
        far = jnp.minimum(near + 1, 3)
        low = x & 127
        wraps = lane < low
        here = []
        for g in range(4):
            upper = jnp.where(
                wraps, wide[z, far, pl.ds(y + 8 * g, 8), :], wide[z, near, pl.ds(y + 8 * g, 8), :]
            )
            lower = jnp.where(
                wraps,
                wide[z, far, pl.ds(y + (8 * g + 1), 8), :],
                wide[z, near, pl.ds(y + (8 * g + 1), 8), :],
            )
            mixed = (1.0 - a) * upper + a * lower
            here.append(pltpu.roll(mixed, (32 * g + 128 - low) & 127, 1))
        left = by_index(group, here)
        spill = by_index(group, here[3:] + here[:3])
        right = pltpu.roll(jnp.where(starts, spill, left), 127, 1)
        value = (1.0 - b) * left + b * right
        zs = z * 2 + slot
        ready[q, zs] = value.astype(BF16)
        kept[q, zs] = value if zs == 0 else pltpu.roll(value, 32 * zs, 1)

    sub = iota((8, 128), 0)
    which = jnp.where(sub < 4, group, (group + 1) & 3)

    def finish(batch):
        @pl.loop(0, BATCH, unroll=HALO_UNROLL)
        def _(step):
            q = batch * BATCH + step
            after = jnp.minimum(q + 1, parts - 1)
            before = jnp.maximum(q - 1, 0)
            both = [
                jnp.where(sub < 4, kept[after, zs], kept[before, zs]) for zs in range(2 * sections)
            ]
            ready[q, 2 * sections] = by_index(which, both).astype(BF16)

        sending(batch).start()

    def sending(batch):
        strips = pl.ds(batch * BATCH, BATCH)
        return pltpu.make_async_copy(ready.at[strips], out.at[strips], sent.at[batch])

    batches = parts // BATCH

    @pl.loop(0, batches)
    def _(batch):
        @pl.loop(0, BATCH, unroll=MAIN_UNROLL)
        def _(step):
            for z in range(sections):
                for slot in range(2):
                    one(batch * BATCH + step, z, slot)

        @pl.when(batch > 0)
        def _():
            finish(batch - 1)

    finish(batches - 1)

    @pl.loop(0, batches)
    def _(batch):
        sending(batch).wait()


def assemble_kernel(table, pool, image):
    me = lax.axis_index("xy")
    bottom = lax.axis_size("xy") - 1
    lane = iota((8, 128), 1)
    group = lane // 32
    sections = image.shape[0]

    def entry(z, strip, s):
        packed = table[(z * 3 + strip) * 32 + s]
        return packed >> 1, 2 * z + (packed & 1)

    for z in range(sections):
        for c in range(4):
            rows = []
            heads, feet = [], []
            for v in range(4):
                k, zs = entry(z, 0, 16 + 4 * c + v)
                piece = pool[k, 4].astype(F32)
                heads.append(pltpu.roll(piece, (32 * (v - zs - 3) + 256) & 127, 1))
                k, zs = entry(z, 2, 4 * c + v)
                piece = pool[k, 4].astype(F32)
                feet.append(pltpu.roll(piece, (32 * (v - zs) + 256) & 127, 1))
            rows.append(jnp.where(me == 0, 0.0, by_index(group, heads)))
            for u in range(2):
                blocks = []
                for v in range(4):
                    k, zs = entry(z, 1, 16 * u + 4 * c + v)
                    blocks.append(pool[k, zs].astype(F32))
                for g in range(4):
                    turned = [
                        blocks[v] if v == g else pltpu.roll(blocks[v], (32 * (v - g)) % 128, 1)
                        for v in range(4)
                    ]
                    rows.append(by_index(group, turned))
            rows.append(jnp.where(me == bottom, 0.0, by_index(group, feet)))
            strip = jnp.concatenate(rows, axis=0)[4:76]
            image[z, :, 128 * c : 128 * c + 128] = strip.astype(BF16)


def band_kernel(bias_one, bias_two, flat_one, flat_two, one, two, gain, lift):
    row = iota(gain.shape, 0)
    gain[...] = by_index(row, [bias_one[o] for o in range(8)])
    row = iota(lift.shape, 0) // 8
    lift[...] = by_index(row, [bias_two[o] for o in range(8)])
    rows, cols = one.shape
    col = iota((27, cols), 1)
    base = (col // WIN_ROWS) % 3 * 9 + col // (3 * WIN_ROWS)
    offset = iota((rows, cols), 1) % WIN_ROWS - iota((rows, cols), 0) // 8
    total = jnp.zeros((rows, cols), F32)
    for e in range(3):
        picks = (iota((27, cols), 0) == base + 3 * e).astype(F32).astype(BF16)
        taps = jnp.dot(flat_one[...], picks, preferred_element_type=F32)
        total = jnp.where(offset == e, jnp.concatenate([taps] * (rows // 8), axis=0), total)
    one[...] = total.astype(BF16)

    rows, cols = two.shape
    col = iota((216, cols), 1)
    base = col % 8 * 27 + col // 80 * 9
    spread = (iota((rows, 24), 0) // 8 == iota((rows, 24), 1)).astype(F32).astype(BF16)
    offset = iota((rows, cols), 1) % 80 // 8 - iota((rows, cols), 0) % 8
    total = jnp.zeros((rows, cols), F32)
    for e in range(3):
        parts = []
        for f in range(3):
            picks = (iota((216, cols), 0) == base + (3 * e + f)).astype(F32).astype(BF16)
            parts.append(jnp.dot(flat_two[...], picks, preferred_element_type=F32))
        taps = jnp.concatenate(parts, axis=0).astype(BF16)
        total = jnp.where(offset == e, jnp.dot(spread, taps, preferred_element_type=F32), total)
    two[...] = total.astype(BF16)


def conv_kernel(
    gain_in, lift_in, before, own, after, one, two, out, shifted, hidden, stage, sent
):
    me, deep = lax.axis_index("xy"), lax.axis_index("gz")
    bottom, last = lax.axis_size("xy") - 1, lax.axis_size("gz") - 1
    lane = iota((IMG_ROWS, W), 1)
    for number, (ref, z) in enumerate(
        [(before, 0), (before, 1), (own, 0), (own, 1), (after, 0), (after, 1)]
    ):
        plane = ref[z].astype(F32)
        if number < 2:
            plane = jnp.where(deep == 0, 0.0, plane)
        if number >= 4:
            plane = jnp.where(deep == last, 0.0, plane)
        shifted[number, 0] = jnp.where(lane == 0, 0.0, pltpu.roll(plane, 1, 1))
        shifted[number, 1] = plane
        shifted[number, 2] = jnp.where(lane == W - 1, 0.0, pltpu.roll(plane, W - 1, 1))
    gain = jnp.concatenate([gain_in[...]] * 4, axis=1)
    lift = jnp.concatenate([lift_in[...]] * 4, axis=1)
    height = HID_ROWS * 8

    @pl.loop(0, 4, unroll=UNROLL_ONE)
    def _(p):
        for b in range(3):
            start = HID_ROWS * b + 2
            stack = jnp.concatenate(
                [
                    shifted[p + d, f, start : start + WIN_ROWS, :]
                    for f in range(3)
                    for d in range(3)
                ],
                axis=0,
            ).astype(BF16)
            total = jnp.dot(one[...], stack, preferred_element_type=F32)
            total = jnp.maximum(total.reshape(HID_ROWS, 8, W) + gain, 0.0)
            keep = jnp.logical_and(
                jnp.logical_or(p > 0, deep > 0), jnp.logical_or(p < 3, deep < last)
            )
            layers = [total[r] for r in range(HID_ROWS)]
            if b == 0:
                layers[0] = jnp.where(me > 0, layers[0], 0.0)
            if b == 2:
                layers[-1] = jnp.where(me < bottom, layers[-1], 0.0)
            total = jnp.where(keep, jnp.concatenate(layers, axis=0), 0.0)
            hidden[p, height * b : height * b + height, :] = total.astype(BF16)

    edge = iota((64, W), 1)

    def sending(z, pair):
        rows = pl.ds(pl.multiple_of(16 * pair, 16), 16)
        return pltpu.make_async_copy(
            stage.at[:, z, rows, :], out.at[:, z, rows, :], sent.at[4 * z + pair]
        )

    @pl.loop(0, 8, unroll=UNROLL_TWO)
    def _(turn):
        z = turn >> 2
        pair = turn & 3
        halves = []
        for b in range(2):
            rows = pl.ds(pl.multiple_of(128 * pair + 64 * b, 64), 80)
            stack = jnp.concatenate([hidden[z + d, rows, :] for d in range(3)], axis=0)
            total = jnp.dot(two[...], stack, preferred_element_type=F32)
            left = jnp.where(edge == 0, 0.0, pltpu.roll(total[0:64], 1, 1))
            right = jnp.where(edge == W - 1, 0.0, pltpu.roll(total[128:192], W - 1, 1))
            halves.append(total[64:128] + left + right + lift)
        rows = pl.ds(pl.multiple_of(16 * pair, 16), 16)
        for o in range(8):
            both = jnp.concatenate([half[8 * o : 8 * o + 8] for half in halves], axis=0)
            stage[o, z, rows, :] = both.astype(BF16)
        sending(z, pair).start()

    @pl.loop(0, 8)
    def _(turn):
        sending(turn >> 2, turn & 3).wait()


def smem():
    return pl.BlockSpec(memory_space=pltpu.SMEM)


def vmem():
    return pl.BlockSpec(memory_space=pltpu.VMEM)


def in_vmem(array):
    return pltpu.with_memory_space_constraint(array, pltpu.VMEM)


def in_smem(array):
    return pltpu.with_memory_space_constraint(array, pltpu.SMEM)


def on_device(
    raw_tiles,
    src_tile,
    shift_y,
    shift_x,
    subpixel,
    owner_map,
    weight_one,
    bias_one,
    weight_two,
    bias_two,
):
    parts = lax.axis_size("xy")
    depth = lax.axis_size("gz")
    me = lax.axis_index("xy")
    deep = lax.axis_index("gz")
    sections = raw_tiles.shape[0]
    source = src_tile.reshape(sections, parts, 32)
    tile_ids = jnp.arange(parts, dtype=jnp.int32)
    number = jnp.arange(32, dtype=jnp.int32)

    outgoing = pl.pallas_call(
        render_kernel,
        out_shape=jax.ShapeDtypeStruct((parts, 5, 8, 128), BF16),
        in_specs=[pl.BlockSpec(memory_space=pl.ANY)] * 6,
        out_specs=pl.BlockSpec(memory_space=pl.ANY),
        scratch_shapes=[
            pltpu.SMEM((parts,), jnp.int32),
            pltpu.VMEM((sections, 1, parts * 32), jnp.int32),
            pltpu.VMEM((sections, parts * 32), jnp.int32),
            pltpu.VMEM((sections, parts * 32), jnp.int32),
            pltpu.VMEM((sections, parts * 32), jnp.int32),
            pltpu.VMEM((sections, 512, 512), BF16),
            pltpu.VMEM((sections, 4, 512, 128), F32),
            pltpu.VMEM((parts, 2 * sections, 8, 128), F32),
            pltpu.VMEM((parts, 5, 8, 128), BF16),
            pltpu.VMEM((8, 128), jnp.int32),
            pltpu.SMEM((8, 128), jnp.int32),
            pltpu.SemaphoreType.DMA((5,)),
            pltpu.SemaphoreType.DMA((2 * sections,)),
            pltpu.SemaphoreType.DMA((1,)),
            pltpu.SemaphoreType.DMA((parts // BATCH,)),
        ],
        name="render",
    )(
        owner_map,
        src_tile.reshape(sections, 1, parts * 32),
        shift_y,
        shift_x,
        subpixel,
        raw_tiles.reshape(sections, 512, 512),
    )

    received = lax.all_to_all(outgoing, "xy", split_axis=0, concat_axis=0, tiled=True)

    around = jnp.clip(me + jnp.arange(-1, 2, dtype=jnp.int32), 0, parts - 1)
    near = jnp.sum(
        jnp.where(
            around[None, :, None, None] == tile_ids[None, None, :, None], source[:, None], 0
        ),
        axis=2,
    )
    holder = jnp.sum(jnp.where(near[..., None] == tile_ids, owner_map, 0), axis=-1)
    second = jnp.any(
        jnp.logical_and(
            near[..., :, None] == near[..., None, :], number[None, :] < number[:, None]
        ),
        axis=-1,
    )
    places = (holder * 2 + second.astype(jnp.int32)).reshape(-1)

    banded_one, banded_two, gain, lift = pl.pallas_call(
        band_kernel,
        out_shape=(
            pltpu.VMEM((HID_ROWS * 8, 9 * WIN_ROWS), BF16),
            pltpu.VMEM((192, 240), BF16),
            pltpu.VMEM((8, 128), F32),
            pltpu.VMEM((64, 128), F32),
        ),
        in_specs=[smem(), smem(), vmem(), vmem()],
        out_specs=(vmem(),) * 4,
        name="bands",
    )(bias_one, bias_two, weight_one.reshape(8, 27), weight_two.reshape(8, 216))

    received, places, banded_one, banded_two, gain, lift = lax.optimization_barrier(
        (received, places, banded_one, banded_two, gain, lift)
    )
    image = pl.pallas_call(
        assemble_kernel,
        out_shape=pltpu.VMEM((sections, IMG_ROWS, W), BF16),
        in_specs=[smem(), vmem()],
        out_specs=vmem(),
        name="assemble",
    )(in_smem(places), in_vmem(received))

    before = lax.ppermute(image, "gz", [(i, (i + 1) % depth) for i in range(depth)])
    after = lax.ppermute(image, "gz", [((i + 1) % depth, i) for i in range(depth)])

    return pl.pallas_call(
        conv_kernel,
        out_shape=jax.ShapeDtypeStruct((8, sections, 64, W), BF16),
        in_specs=[vmem()] * 7,
        out_specs=pl.BlockSpec(memory_space=pl.ANY),
        scratch_shapes=[
            pltpu.VMEM((6, 3, IMG_ROWS, W), F32),
            pltpu.VMEM((4, 66 * 8, W), BF16),
            pltpu.VMEM((8, sections, 64, W), BF16),
            pltpu.SemaphoreType.DMA((4 * sections,)),
        ],
        name="convolve",
    )(
        in_vmem(gain),
        in_vmem(lift),
        in_vmem(before),
        in_vmem(image),
        in_vmem(after),
        in_vmem(banded_one),
        in_vmem(banded_two),
    )


def solution(mesh):
    in_specs = (
        P("gz", "xy", None, None),
        P("gz", None, None),
        P("gz", None),
        P("gz", None),
        P("gz", None),
        P(),
        P(),
        P(),
        P(),
        P(),
    )
    out_specs = P(None, "gz", "xy", None)
    return jax.shard_map(
        on_device, mesh=mesh, in_specs=in_specs, out_specs=out_specs, check_vma=False
    )
```

```python
import jax
import jax.numpy as jnp
from jax import lax
from jax.experimental import pallas as pl
from jax.experimental.pallas import tpu as pltpu
from jax.sharding import PartitionSpec as P

SUB = 32
W = 512
HID_ROWS = 22
WIN_ROWS = 24
IMG_ROWS = 72
BATCH = 8
MAIN_UNROLL = 8
HALO_UNROLL = 4
UNROLL_TWO = 8
F32 = jnp.float32
BF16 = jnp.bfloat16


def iota(shape, dim):
    return lax.broadcasted_iota(jnp.int32, shape, dim)


def by_index(which, choices):
    result = choices[-1]
    for number in range(len(choices) - 2, -1, -1):
        result = jnp.where(which == number, choices[number], result)
    return result


def step_right(block):
    first = iota((block.shape[0], 128), 1) == 0
    turned = [pltpu.roll(block[:, c : c + 128], 1, 1) for c in range(0, W, 128)]
    before = [0.0] + turned[:-1]
    return jnp.concatenate([jnp.where(first, x, y) for x, y in zip(before, turned)], axis=1)


def step_left(block):
    final = iota((block.shape[0], 128), 1) == 127
    turned = [pltpu.roll(block[:, c : c + 128], 127, 1) for c in range(0, W, 128)]
    after = turned[1:] + [0.0]
    return jnp.concatenate([jnp.where(final, x, y) for x, y in zip(after, turned)], axis=1)


def render_kernel(
    owner_in,
    source_in,
    tops_in,
    lefts_in,
    codes_in,
    tiles,
    out,
    owner,
    source,
    tops,
    lefts,
    codes,
    landing,
    wide,
    kept,
    ready,
    found,
    table,
    arrived,
    landed,
    listed,
    sent,
):
    parts = out.shape[0]
    sections = tiles.shape[0]
    small = [
        pltpu.make_async_copy(src, dst, arrived.at[n])
        for n, (src, dst) in enumerate(
            [
                (source_in, source),
                (owner_in, owner),
                (tops_in, tops),
                (lefts_in, lefts),
                (codes_in, codes),
            ]
        )
    ]
    half = landing.shape[1] // 2
    copies = [
        pltpu.make_async_copy(
            tiles.at[z, pl.ds(half * h, half), :],
            landing.at[z, pl.ds(half * h, half), :],
            landed.at[2 * z + h],
        )
        for z in range(sections)
        for h in range(2)
    ]
    for copy in small + copies:
        copy.start()
    count = source.shape[2]
    early, late = iota((128, 128), 0), iota((128, 128), 1)
    upto = jnp.logical_and(early // 32 == late // 32, early <= late).astype(F32).astype(BF16)
    strips = (iota((count, 128), 0) // 32 == iota((count, 128), 1)).astype(F32).astype(BF16)
    for copy in small[:2]:
        copy.wait()

    me = lax.axis_index("xy")
    mine = jnp.int32(0)
    for k in range(parts):
        mine = jnp.where(owner[k] == me, k, mine)
    blank = jnp.full((8 - sections, count), -1, jnp.int32)
    match = jnp.concatenate([source[z] for z in range(sections)] + [blank], axis=0) == mine
    marks = match.astype(F32)
    tall = jnp.concatenate([marks[:, t : t + 128] for t in range(0, count, 128)], axis=0)
    ranks = jnp.dot(tall.astype(BF16), upto, preferred_element_type=F32)
    rank = jnp.concatenate([ranks[t : t + 8] for t in range(0, count // 16, 8)], axis=1)
    for copy in small[2:]:
        copy.wait()
    packed = tops[...] + (lefts[...] << 9) + (codes[...] << 18)
    packed = jnp.concatenate([packed, blank], axis=0)
    pieces = []
    for slot in range(2):
        chosen = jnp.where(jnp.logical_and(match, rank == slot + 1), packed, 0)
        for k in range(3):
            pieces.append(((chosen >> (8 * k)) & 255).astype(F32))
    sums = jnp.dot(
        jnp.concatenate(pieces, axis=0).astype(BF16), strips, preferred_element_type=F32
    ).astype(jnp.int32)
    pair = [
        sums[24 * slot : 24 * slot + 8]
        + (sums[24 * slot + 8 : 24 * slot + 16] << 8)
        + (sums[24 * slot + 16 : 24 * slot + 24] << 16)
        for slot in range(2)
    ]
    found[...] = jnp.where(iota((8, 128), 0) < 2, pair[0], pltpu.roll(pair[1], 2, 0))
    listing = pltpu.make_async_copy(found, table, listed.at[0])
    listing.start()

    for z in range(sections):
        for h in range(2):
            copies[2 * z + h].wait()
            rows = pl.ds(half * h, half)
            for t in range(4):
                wide[z, t, rows, :] = landing[z, rows, 128 * t : 128 * t + 128].astype(F32)
    listing.wait()
    lane = iota((8, 128), 1)
    group = lane // 32
    starts = lane % 32 == 0

    def one(q, z, slot):
        code = table[2 * slot + z, q]
        y = code & 511
        x = (code >> 9) & 511
        a = ((code >> 20) & 3).astype(F32) * 0.25
        b = ((code >> 18) & 3).astype(F32) * 0.25
        near = x >> 7
        far = jnp.minimum(near + 1, 3)
        low = x & 127
        wraps = lane < low
        here = []
        for g in range(4):
            upper = jnp.where(
                wraps, wide[z, far, pl.ds(y + 8 * g, 8), :], wide[z, near, pl.ds(y + 8 * g, 8), :]
            )
            lower = jnp.where(
                wraps,
                wide[z, far, pl.ds(y + (8 * g + 1), 8), :],
                wide[z, near, pl.ds(y + (8 * g + 1), 8), :],
            )
            mixed = (1.0 - a) * upper + a * lower
            here.append(mixed if g == 0 else pltpu.roll(mixed, 32 * g, 1))
        turn = (lane - low) & 127
        left = by_index(turn >> 5, here)
        spill = by_index(turn >> 5, here[3:] + here[:3])
        right = pltpu.roll(jnp.where((turn & 31) == 0, spill, left), 127, 1)
        value = (1.0 - b) * left + b * right
        zs = z * 2 + slot
        ready[q, zs] = pltpu.roll(value, (128 - low) & 127, 1).astype(BF16)
        kept[q, zs] = pltpu.roll(value, (32 * zs + 128 - low) & 127, 1)

    sub = iota((8, 128), 0)
    which = jnp.where(sub < 4, group, (group + 1) & 3)

    def finish(batch):
        @pl.loop(0, BATCH, unroll=HALO_UNROLL)
        def _(step):
            q = batch * BATCH + step
            after = jnp.minimum(q + 1, parts - 1)
            before = jnp.maximum(q - 1, 0)
            both = [
                jnp.where(sub < 4, kept[after, zs], kept[before, zs]) for zs in range(2 * sections)
            ]
            ready[q, 2 * sections] = by_index(which, both).astype(BF16)

        sending(batch).start()

    def sending(batch):
        strips = pl.ds(batch * BATCH, BATCH)
        return pltpu.make_async_copy(ready.at[strips], out.at[strips], sent.at[batch])

    batches = parts // BATCH

    @pl.loop(0, batches)
    def _(batch):
        @pl.loop(0, BATCH, unroll=MAIN_UNROLL)
        def _(step):
            for z in range(sections):
                for slot in range(2):
                    one(batch * BATCH + step, z, slot)

        @pl.when(batch > 0)
        def _():
            finish(batch - 1)

    finish(batches - 1)

    @pl.loop(0, batches)
    def _(batch):
        sending(batch).wait()


def assemble_kernel(table, pool, image):
    me = lax.axis_index("xy")
    bottom = lax.axis_size("xy") - 1
    lane = iota((8, 128), 1)
    group = lane // 32
    sections = image.shape[0]

    def entry(z, strip, s):
        packed = table[(z * 3 + strip) * 32 + s]
        return packed >> 1, 2 * z + (packed & 1)

    for z in range(sections):
        for c in range(4):
            rows = []
            heads, feet = [], []
            for v in range(4):
                k, zs = entry(z, 0, 16 + 4 * c + v)
                piece = pool[k, 4].astype(F32)
                heads.append(pltpu.roll(piece, (32 * (v - zs - 3) + 256) & 127, 1))
                k, zs = entry(z, 2, 4 * c + v)
                piece = pool[k, 4].astype(F32)
                feet.append(pltpu.roll(piece, (32 * (v - zs) + 256) & 127, 1))
            rows.append(jnp.where(me == 0, 0.0, by_index(group, heads)))
            for u in range(2):
                blocks = []
                for v in range(4):
                    k, zs = entry(z, 1, 16 * u + 4 * c + v)
                    blocks.append(pool[k, zs].astype(F32))
                for g in range(4):
                    turned = [
                        blocks[v] if v == g else pltpu.roll(blocks[v], (32 * (v - g)) % 128, 1)
                        for v in range(4)
                    ]
                    rows.append(by_index(group, turned))
            rows.append(jnp.where(me == bottom, 0.0, by_index(group, feet)))
            strip = jnp.concatenate(rows, axis=0)[4:76]
            image[z, :, 128 * c : 128 * c + 128] = strip.astype(BF16)


def band_kernel(bias_one, bias_two, flat_one, flat_two, one, two, gain, lift):
    row = iota(gain.shape, 0)
    gain[...] = by_index(row, [bias_one[o] for o in range(8)])
    row = iota(lift.shape, 0) // 8
    lift[...] = by_index(row, [bias_two[o] for o in range(8)])
    rows, cols = one.shape
    col = iota((27, cols), 1)
    base = (col // WIN_ROWS) % 3 * 9 + col // (3 * WIN_ROWS)
    offset = iota((rows, cols), 1) % WIN_ROWS - iota((rows, cols), 0) // 8
    total = jnp.zeros((rows, cols), F32)
    for e in range(3):
        picks = (iota((27, cols), 0) == base + 3 * e).astype(F32).astype(BF16)
        taps = jnp.dot(flat_one[...], picks, preferred_element_type=F32)
        total = jnp.where(offset == e, jnp.concatenate([taps] * (rows // 8), axis=0), total)
    one[...] = total.astype(BF16)

    rows, cols = two.shape
    col = iota((216, cols), 1)
    base = col % 8 * 27 + col // 80 * 9
    spread = (iota((rows, 24), 0) // 8 == iota((rows, 24), 1)).astype(F32).astype(BF16)
    offset = iota((rows, cols), 1) % 80 // 8 - iota((rows, cols), 0) % 8
    total = jnp.zeros((rows, cols), F32)
    for e in range(3):
        parts = []
        for f in range(3):
            picks = (iota((216, cols), 0) == base + (3 * e + f)).astype(F32).astype(BF16)
            parts.append(jnp.dot(flat_two[...], picks, preferred_element_type=F32))
        taps = jnp.concatenate(parts, axis=0).astype(BF16)
        total = jnp.where(offset == e, jnp.dot(spread, taps, preferred_element_type=F32), total)
    two[...] = total.astype(BF16)


def conv_kernel(
    gain_in, lift_in, before, own, after, one, two, out, shifted, hidden, stage, sent
):
    me, deep = lax.axis_index("xy"), lax.axis_index("gz")
    bottom, last = lax.axis_size("xy") - 1, lax.axis_size("gz") - 1
    for number, (ref, z) in enumerate(
        [(before, 0), (before, 1), (own, 0), (own, 1), (after, 0), (after, 1)]
    ):
        plane = ref[z].astype(F32)
        if number < 2:
            plane = jnp.where(deep == 0, 0.0, plane)
        if number >= 4:
            plane = jnp.where(deep == last, 0.0, plane)
        shifted[number, 0] = step_right(plane)
        shifted[number, 1] = plane
        shifted[number, 2] = step_left(plane)
    gain = jnp.concatenate([gain_in[...]] * 4, axis=1)
    lift = jnp.concatenate([lift_in[...]] * 4, axis=1)
    height = HID_ROWS * 8

    for p in range(4):
        weight, bias = one[...], gain
        if p == 0:
            weight, bias = jnp.where(deep > 0, weight, 0), jnp.where(deep > 0, gain, 0.0)
        if p == 3:
            weight, bias = jnp.where(deep < last, weight, 0), jnp.where(deep < last, gain, 0.0)
        for b in range(3):
            start = HID_ROWS * b + 2
            stack = jnp.concatenate(
                [
                    shifted[p + d, f, start : start + WIN_ROWS, :]
                    for f in range(3)
                    for d in range(3)
                ],
                axis=0,
            ).astype(BF16)
            total = jnp.dot(weight, stack, preferred_element_type=F32)
            total = jnp.maximum(total.reshape(HID_ROWS, 8, W) + bias, 0.0)
            layers = [total[r] for r in range(HID_ROWS)]
            if b == 0:
                layers[0] = jnp.where(me > 0, layers[0], 0.0)
            if b == 2:
                layers[-1] = jnp.where(me < bottom, layers[-1], 0.0)
            total = jnp.concatenate(layers, axis=0)
            hidden[p, height * b : height * b + height, :] = total.astype(BF16)


    def sending(z, pair):
        rows = pl.ds(pl.multiple_of(16 * pair, 16), 16)
        return pltpu.make_async_copy(
            stage.at[:, z, rows, :], out.at[:, z, rows, :], sent.at[4 * z + pair]
        )

    @pl.loop(0, 8, unroll=UNROLL_TWO)
    def _(turn):
        z = turn >> 2
        pair = turn & 3
        halves = []
        for b in range(2):
            rows = pl.ds(pl.multiple_of(128 * pair + 64 * b, 64), 80)
            stack = jnp.concatenate([hidden[z + d, rows, :] for d in range(3)], axis=0)
            total = jnp.dot(two[...], stack, preferred_element_type=F32)
            left, right = step_right(total[0:64]), step_left(total[128:192])
            halves.append(total[64:128] + left + right + lift)
        rows = pl.ds(pl.multiple_of(16 * pair, 16), 16)
        for o in range(8):
            both = jnp.concatenate([half[8 * o : 8 * o + 8] for half in halves], axis=0)
            stage[o, z, rows, :] = both.astype(BF16)
        sending(z, pair).start()

    @pl.loop(0, 8)
    def _(turn):
        sending(turn >> 2, turn & 3).wait()


def smem():
    return pl.BlockSpec(memory_space=pltpu.SMEM)


def vmem():
    return pl.BlockSpec(memory_space=pltpu.VMEM)


def in_vmem(array):
    return pltpu.with_memory_space_constraint(array, pltpu.VMEM)


def in_smem(array):
    return pltpu.with_memory_space_constraint(array, pltpu.SMEM)


def on_device(
    raw_tiles,
    src_tile,
    shift_y,
    shift_x,
    subpixel,
    owner_map,
    weight_one,
    bias_one,
    weight_two,
    bias_two,
):
    parts = lax.axis_size("xy")
    depth = lax.axis_size("gz")
    me = lax.axis_index("xy")
    deep = lax.axis_index("gz")
    sections = raw_tiles.shape[0]
    source = src_tile.reshape(sections, parts, 32)
    tile_ids = jnp.arange(parts, dtype=jnp.int32)
    number = jnp.arange(32, dtype=jnp.int32)

    outgoing = pl.pallas_call(
        render_kernel,
        out_shape=jax.ShapeDtypeStruct((parts, 5, 8, 128), BF16),
        in_specs=[pl.BlockSpec(memory_space=pl.ANY)] * 6,
        out_specs=pl.BlockSpec(memory_space=pl.ANY),
        scratch_shapes=[
            pltpu.SMEM((parts,), jnp.int32),
            pltpu.VMEM((sections, 1, parts * 32), jnp.int32),
            pltpu.VMEM((sections, parts * 32), jnp.int32),
            pltpu.VMEM((sections, parts * 32), jnp.int32),
            pltpu.VMEM((sections, parts * 32), jnp.int32),
            pltpu.VMEM((sections, 512, 512), BF16),
            pltpu.VMEM((sections, 4, 512, 128), F32),
            pltpu.VMEM((parts, 2 * sections, 8, 128), F32),
            pltpu.VMEM((parts, 5, 8, 128), BF16),
            pltpu.VMEM((8, 128), jnp.int32),
            pltpu.SMEM((8, 128), jnp.int32),
            pltpu.SemaphoreType.DMA((5,)),
            pltpu.SemaphoreType.DMA((2 * sections,)),
            pltpu.SemaphoreType.DMA((1,)),
            pltpu.SemaphoreType.DMA((parts // BATCH,)),
        ],
        name="render",
    )(
        owner_map,
        src_tile.reshape(sections, 1, parts * 32),
        shift_y,
        shift_x,
        subpixel,
        raw_tiles.reshape(sections, 512, 512),
    )

    received = lax.all_to_all(outgoing, "xy", split_axis=0, concat_axis=0, tiled=True)

    around = jnp.clip(me + jnp.arange(-1, 2, dtype=jnp.int32), 0, parts - 1)
    near = jnp.sum(
        jnp.where(
            around[None, :, None, None] == tile_ids[None, None, :, None], source[:, None], 0
        ),
        axis=2,
    )
    holder = jnp.sum(jnp.where(near[..., None] == tile_ids, owner_map, 0), axis=-1)
    second = jnp.any(
        jnp.logical_and(
            near[..., :, None] == near[..., None, :], number[None, :] < number[:, None]
        ),
        axis=-1,
    )
    places = (holder * 2 + second.astype(jnp.int32)).reshape(-1)

    banded_one, banded_two, gain, lift = pl.pallas_call(
        band_kernel,
        out_shape=(
            pltpu.VMEM((HID_ROWS * 8, 9 * WIN_ROWS), BF16),
            pltpu.VMEM((192, 240), BF16),
            pltpu.VMEM((8, 128), F32),
            pltpu.VMEM((64, 128), F32),
        ),
        in_specs=[smem(), smem(), vmem(), vmem()],
        out_specs=(vmem(),) * 4,
        name="bands",
    )(bias_one, bias_two, weight_one.reshape(8, 27), weight_two.reshape(8, 216))

    received, places, banded_one, banded_two, gain, lift = lax.optimization_barrier(
        (received, places, banded_one, banded_two, gain, lift)
    )
    image = pl.pallas_call(
        assemble_kernel,
        out_shape=pltpu.VMEM((sections, IMG_ROWS, W), BF16),
        in_specs=[smem(), vmem()],
        out_specs=vmem(),
        compiler_params=pltpu.CompilerParams(vmem_limit_bytes=32 << 20),
        name="assemble",
    )(in_smem(places), in_vmem(received))

    before = lax.ppermute(image, "gz", [(i, (i + 1) % depth) for i in range(depth)])
    after = lax.ppermute(image, "gz", [((i + 1) % depth, i) for i in range(depth)])

    return pl.pallas_call(
        conv_kernel,
        out_shape=jax.ShapeDtypeStruct((8, sections, 64, W), BF16),
        in_specs=[vmem()] * 7,
        out_specs=pl.BlockSpec(memory_space=pl.ANY),
        scratch_shapes=[
            pltpu.VMEM((6, 3, IMG_ROWS, W), F32),
            pltpu.VMEM((4, 66 * 8, W), BF16),
            pltpu.VMEM((8, sections, 64, W), BF16),
            pltpu.SemaphoreType.DMA((4 * sections,)),
        ],
        name="convolve",
    )(
        in_vmem(gain),
        in_vmem(lift),
        in_vmem(before),
        in_vmem(image),
        in_vmem(after),
        in_vmem(banded_one),
        in_vmem(banded_two),
    )


def solution(mesh):
    in_specs = (
        P("gz", "xy", None, None),
        P("gz", None, None),
        P("gz", None),
        P("gz", None),
        P("gz", None),
        P(),
        P(),
        P(),
        P(),
        P(),
    )
    out_specs = P(None, "gz", "xy", None)
    return jax.shard_map(
        on_device, mesh=mesh, in_specs=in_specs, out_specs=out_specs, check_vma=False
    )
```

```python
import jax
import jax.numpy as jnp
from jax import lax
from jax.experimental import pallas as pl
from jax.experimental.pallas import tpu as pltpu
from jax.sharding import PartitionSpec as P

SUB = 32
W = 512
HID_ROWS = 22
WIN_ROWS = 24
IMG_ROWS = 72
BATCH = 8
MAIN_UNROLL = 8
HALO_UNROLL = 4
F32 = jnp.float32
BF16 = jnp.bfloat16


def iota(shape, dim):
    return lax.broadcasted_iota(jnp.int32, shape, dim)


def by_index(which, choices):
    result = choices[-1]
    for number in range(len(choices) - 2, -1, -1):
        result = jnp.where(which == number, choices[number], result)
    return result


def step_right(block):
    first = iota((block.shape[0], 128), 1) == 0
    turned = [pltpu.roll(block[:, c : c + 128], 1, 1) for c in range(0, W, 128)]
    before = [0.0] + turned[:-1]
    return jnp.concatenate([jnp.where(first, x, y) for x, y in zip(before, turned)], axis=1)


def step_left(block):
    final = iota((block.shape[0], 128), 1) == 127
    turned = [pltpu.roll(block[:, c : c + 128], 127, 1) for c in range(0, W, 128)]
    after = turned[1:] + [0.0]
    return jnp.concatenate([jnp.where(final, x, y) for x, y in zip(after, turned)], axis=1)


def render_kernel(
    owner_in,
    source_in,
    tops_in,
    lefts_in,
    codes_in,
    tiles,
    out,
    owner,
    source,
    tops,
    lefts,
    codes,
    landing,
    wide,
    kept,
    ready,
    found,
    table,
    arrived,
    landed,
    listed,
    sent,
):
    parts = out.shape[0]
    sections = tiles.shape[0]
    small = [
        pltpu.make_async_copy(src, dst, arrived.at[n])
        for n, (src, dst) in enumerate(
            [
                (source_in, source),
                (owner_in, owner),
                (tops_in, tops),
                (lefts_in, lefts),
                (codes_in, codes),
            ]
        )
    ]
    half = landing.shape[1] // 2
    copies = [
        pltpu.make_async_copy(
            tiles.at[z, pl.ds(half * h, half), :],
            landing.at[z, pl.ds(half * h, half), :],
            landed.at[2 * z + h],
        )
        for z in range(sections)
        for h in range(2)
    ]
    for copy in small + copies:
        copy.start()
    count = source.shape[2]
    early, late = iota((128, 128), 0), iota((128, 128), 1)
    upto = jnp.logical_and(early // 32 == late // 32, early <= late).astype(F32).astype(BF16)
    strips = (iota((count, 128), 0) // 32 == iota((count, 128), 1)).astype(F32).astype(BF16)
    for copy in small[:2]:
        copy.wait()

    me = lax.axis_index("xy")
    mine = jnp.int32(0)
    for k in range(parts):
        mine = jnp.where(owner[k] == me, k, mine)
    blank = jnp.full((8 - sections, count), -1, jnp.int32)
    match = jnp.concatenate([source[z] for z in range(sections)] + [blank], axis=0) == mine
    marks = match.astype(F32)
    tall = jnp.concatenate([marks[:, t : t + 128] for t in range(0, count, 128)], axis=0)
    ranks = jnp.dot(tall.astype(BF16), upto, preferred_element_type=F32)
    rank = jnp.concatenate([ranks[t : t + 8] for t in range(0, count // 16, 8)], axis=1)
    for copy in small[2:]:
        copy.wait()
    packed = tops[...] + (lefts[...] << 9) + (codes[...] << 18)
    packed = jnp.concatenate([packed, blank], axis=0)
    pieces = []
    for slot in range(2):
        chosen = jnp.where(jnp.logical_and(match, rank == slot + 1), packed, 0)
        for k in range(3):
            pieces.append(((chosen >> (8 * k)) & 255).astype(F32))
    sums = jnp.dot(
        jnp.concatenate(pieces, axis=0).astype(BF16), strips, preferred_element_type=F32
    ).astype(jnp.int32)
    pair = [
        sums[24 * slot : 24 * slot + 8]
        + (sums[24 * slot + 8 : 24 * slot + 16] << 8)
        + (sums[24 * slot + 16 : 24 * slot + 24] << 16)
        for slot in range(2)
    ]
    found[...] = jnp.where(iota((8, 128), 0) < 2, pair[0], pltpu.roll(pair[1], 2, 0))
    listing = pltpu.make_async_copy(found, table, listed.at[0])
    listing.start()

    for z in range(sections):
        for h in range(2):
            copies[2 * z + h].wait()
            rows = pl.ds(half * h, half)
            for t in range(4):
                wide[z, t, rows, :] = landing[z, rows, 128 * t : 128 * t + 128].astype(F32)
    listing.wait()
    lane = iota((8, 128), 1)
    group = lane // 32
    starts = lane % 32 == 0

    def one(q, z, slot):
        code = table[2 * slot + z, q]
        y = code & 511
        x = (code >> 9) & 511
        a = ((code >> 20) & 3).astype(F32) * 0.25
        b = ((code >> 18) & 3).astype(F32) * 0.25
        near = x >> 7
        far = jnp.minimum(near + 1, 3)
        low = x & 127
        wraps = lane < low
        here = []
        for g in range(4):
            upper = jnp.where(
                wraps, wide[z, far, pl.ds(y + 8 * g, 8), :], wide[z, near, pl.ds(y + 8 * g, 8), :]
            )
            lower = jnp.where(
                wraps,
                wide[z, far, pl.ds(y + (8 * g + 1), 8), :],
                wide[z, near, pl.ds(y + (8 * g + 1), 8), :],
            )
            mixed = (1.0 - a) * upper + a * lower
            here.append(mixed if g == 0 else pltpu.roll(mixed, 32 * g, 1))
        turn = (lane - low) & 127
        left = by_index(turn >> 5, here)
        spill = by_index(turn >> 5, here[3:] + here[:3])
        right = pltpu.roll(jnp.where((turn & 31) == 0, spill, left), 127, 1)
        value = (1.0 - b) * left + b * right
        zs = z * 2 + slot
        ready[q, zs] = pltpu.roll(value, (128 - low) & 127, 1).astype(BF16)
        kept[q, zs] = pltpu.roll(value, (32 * zs + 128 - low) & 127, 1)

    sub = iota((8, 128), 0)
    which = jnp.where(sub < 4, group, (group + 1) & 3)

    def finish(batch):
        @pl.loop(0, BATCH, unroll=HALO_UNROLL)
        def _(step):
            q = batch * BATCH + step
            after = jnp.minimum(q + 1, parts - 1)
            before = jnp.maximum(q - 1, 0)
            both = [
                jnp.where(sub < 4, kept[after, zs], kept[before, zs]) for zs in range(2 * sections)
            ]
            ready[q, 2 * sections] = by_index(which, both).astype(BF16)

        sending(batch).start()

    def sending(batch):
        strips = pl.ds(batch * BATCH, BATCH)
        return pltpu.make_async_copy(ready.at[strips], out.at[strips], sent.at[batch])

    batches = parts // BATCH

    @pl.loop(0, batches)
    def _(batch):
        @pl.loop(0, BATCH, unroll=MAIN_UNROLL)
        def _(step):
            for z in range(sections):
                for slot in range(2):
                    one(batch * BATCH + step, z, slot)

        @pl.when(batch > 0)
        def _():
            finish(batch - 1)

    finish(batches - 1)

    @pl.loop(0, batches)
    def _(batch):
        sending(batch).wait()


def assemble_kernel(table, pool, image):
    me = lax.axis_index("xy")
    bottom = lax.axis_size("xy") - 1
    lane = iota((8, 128), 1)
    group = lane // 32
    sections = image.shape[0]

    def entry(z, strip, s):
        packed = table[(z * 3 + strip) * 32 + s]
        return packed >> 1, 2 * z + (packed & 1)

    for z in range(sections):
        for c in range(4):
            rows = []
            heads, feet = [], []
            for v in range(4):
                k, zs = entry(z, 0, 16 + 4 * c + v)
                piece = pool[k, 4].astype(F32)
                heads.append(pltpu.roll(piece, (32 * (v - zs - 3) + 256) & 127, 1))
                k, zs = entry(z, 2, 4 * c + v)
                piece = pool[k, 4].astype(F32)
                feet.append(pltpu.roll(piece, (32 * (v - zs) + 256) & 127, 1))
            rows.append(jnp.where(me == 0, 0.0, by_index(group, heads)))
            for u in range(2):
                blocks = []
                for v in range(4):
                    k, zs = entry(z, 1, 16 * u + 4 * c + v)
                    blocks.append(pool[k, zs].astype(F32))
                for g in range(4):
                    turned = [
                        blocks[v] if v == g else pltpu.roll(blocks[v], (32 * (v - g)) % 128, 1)
                        for v in range(4)
                    ]
                    rows.append(by_index(group, turned))
            rows.append(jnp.where(me == bottom, 0.0, by_index(group, feet)))
            strip = jnp.concatenate(rows, axis=0)[4:76]
            image[z, :, 128 * c : 128 * c + 128] = strip.astype(BF16)


def band_kernel(bias_one, bias_two, flat_one, flat_two, one, two, gain, lift):
    row = iota(gain.shape, 0)
    gain[...] = by_index(row, [bias_one[o] for o in range(8)])
    row = iota(lift.shape, 0) // 8
    lift[...] = by_index(row, [bias_two[o] for o in range(8)])
    rows, cols = one.shape
    col = iota((27, cols), 1)
    base = (col // WIN_ROWS) % 3 * 9 + col // (3 * WIN_ROWS)
    offset = iota((rows, cols), 1) % WIN_ROWS - iota((rows, cols), 0) // 8
    total = jnp.zeros((rows, cols), F32)
    for e in range(3):
        picks = (iota((27, cols), 0) == base + 3 * e).astype(F32).astype(BF16)
        taps = jnp.dot(flat_one[...], picks, preferred_element_type=F32)
        total = jnp.where(offset == e, jnp.concatenate([taps] * (rows // 8), axis=0), total)
    one[...] = total.astype(BF16)

    rows, cols = two.shape
    col = iota((216, cols), 1)
    base = col % 8 * 27 + col // 80 * 9
    spread = (iota((rows, 24), 0) // 8 == iota((rows, 24), 1)).astype(F32).astype(BF16)
    offset = iota((rows, cols), 1) % 80 // 8 - iota((rows, cols), 0) % 8
    total = jnp.zeros((rows, cols), F32)
    for e in range(3):
        parts = []
        for f in range(3):
            picks = (iota((216, cols), 0) == base + (3 * e + f)).astype(F32).astype(BF16)
            parts.append(jnp.dot(flat_two[...], picks, preferred_element_type=F32))
        taps = jnp.concatenate(parts, axis=0).astype(BF16)
        total = jnp.where(offset == e, jnp.dot(spread, taps, preferred_element_type=F32), total)
    two[...] = total.astype(BF16)


def conv_kernel(
    gain_in, lift_in, before, own, after, one, two, out, shifted, hidden, stage, sent
):
    me, deep = lax.axis_index("xy"), lax.axis_index("gz")
    bottom, last = lax.axis_size("xy") - 1, lax.axis_size("gz") - 1
    for number, (ref, z) in enumerate(
        [(before, 0), (before, 1), (own, 0), (own, 1), (after, 0), (after, 1)]
    ):
        plane = ref[z].astype(F32)
        if number < 2:
            plane = jnp.where(deep == 0, 0.0, plane)
        if number >= 4:
            plane = jnp.where(deep == last, 0.0, plane)
        shifted[number, 0] = step_right(plane)
        shifted[number, 1] = plane
        shifted[number, 2] = step_left(plane)
    gain = jnp.concatenate([gain_in[...]] * 4, axis=1)
    lift = jnp.concatenate([lift_in[...]] * 4, axis=1)
    height = HID_ROWS * 8

    weights, biases = [one[...]] * 4, [gain] * 4
    weights[0], biases[0] = jnp.where(deep > 0, one[...], 0), jnp.where(deep > 0, gain, 0.0)
    weights[3], biases[3] = jnp.where(deep < last, one[...], 0), jnp.where(deep < last, gain, 0.0)

    def first_layer(p, b):
        start = HID_ROWS * b + 2
        stack = jnp.concatenate(
            [
                shifted[p + d, f, start : start + WIN_ROWS, :]
                for f in range(3)
                for d in range(3)
            ],
            axis=0,
        ).astype(BF16)
        total = jnp.dot(weights[p], stack, preferred_element_type=F32)
        total = jnp.maximum(total.reshape(HID_ROWS, 8, W) + biases[p], 0.0)
        layers = [total[r] for r in range(HID_ROWS)]
        if b == 0:
            layers[0] = jnp.where(me > 0, layers[0], 0.0)
        if b == 2:
            layers[-1] = jnp.where(me < bottom, layers[-1], 0.0)
        total = jnp.concatenate(layers, axis=0)
        hidden[p, height * b : height * b + height, :] = total.astype(BF16)

    def second_layer(z, pair):
        halves = []
        for b in (2 * pair, 2 * pair + 1):
            stack = jnp.concatenate(
                [hidden[z + d, 64 * b : 64 * b + 80, :] for d in range(3)], axis=0
            )
            total = jnp.dot(two[...], stack, preferred_element_type=F32)
            left, right = step_right(total[0:64]), step_left(total[128:192])
            halves.append(total[64:128] + left + right + lift)
        rows = pl.ds(16 * pair, 16)
        for o in range(8):
            both = jnp.concatenate([half[8 * o : 8 * o + 8] for half in halves], axis=0)
            stage[o, z, rows, :] = both.astype(BF16)
        copy = pltpu.make_async_copy(
            stage.at[:, z, rows, :], out.at[:, z, rows, :], sent.at[4 * z + pair]
        )
        copy.start()
        return copy

    copies = []
    for b, pairs in enumerate(((0,), (1,), (2, 3))):
        for p in range(4):
            first_layer(p, b)
        copies += [second_layer(z, pair) for pair in pairs for z in range(2)]
    for copy in copies:
        copy.wait()


def smem():
    return pl.BlockSpec(memory_space=pltpu.SMEM)


def vmem():
    return pl.BlockSpec(memory_space=pltpu.VMEM)


def in_vmem(array):
    return pltpu.with_memory_space_constraint(array, pltpu.VMEM)


def in_smem(array):
    return pltpu.with_memory_space_constraint(array, pltpu.SMEM)


def on_device(
    raw_tiles,
    src_tile,
    shift_y,
    shift_x,
    subpixel,
    owner_map,
    weight_one,
    bias_one,
    weight_two,
    bias_two,
):
    parts = lax.axis_size("xy")
    depth = lax.axis_size("gz")
    me = lax.axis_index("xy")
    deep = lax.axis_index("gz")
    sections = raw_tiles.shape[0]
    source = src_tile.reshape(sections, parts, 32)
    tile_ids = jnp.arange(parts, dtype=jnp.int32)
    number = jnp.arange(32, dtype=jnp.int32)

    outgoing = pl.pallas_call(
        render_kernel,
        out_shape=jax.ShapeDtypeStruct((parts, 5, 8, 128), BF16),
        in_specs=[pl.BlockSpec(memory_space=pl.ANY)] * 6,
        out_specs=pl.BlockSpec(memory_space=pl.ANY),
        scratch_shapes=[
            pltpu.SMEM((parts,), jnp.int32),
            pltpu.VMEM((sections, 1, parts * 32), jnp.int32),
            pltpu.VMEM((sections, parts * 32), jnp.int32),
            pltpu.VMEM((sections, parts * 32), jnp.int32),
            pltpu.VMEM((sections, parts * 32), jnp.int32),
            pltpu.VMEM((sections, 512, 512), BF16),
            pltpu.VMEM((sections, 4, 512, 128), F32),
            pltpu.VMEM((parts, 2 * sections, 8, 128), F32),
            pltpu.VMEM((parts, 5, 8, 128), BF16),
            pltpu.VMEM((8, 128), jnp.int32),
            pltpu.SMEM((8, 128), jnp.int32),
            pltpu.SemaphoreType.DMA((5,)),
            pltpu.SemaphoreType.DMA((2 * sections,)),
            pltpu.SemaphoreType.DMA((1,)),
            pltpu.SemaphoreType.DMA((parts // BATCH,)),
        ],
        name="render",
    )(
        owner_map,
        src_tile.reshape(sections, 1, parts * 32),
        shift_y,
        shift_x,
        subpixel,
        raw_tiles.reshape(sections, 512, 512),
    )

    received = lax.all_to_all(outgoing, "xy", split_axis=0, concat_axis=0, tiled=True)

    around = jnp.clip(me + jnp.arange(-1, 2, dtype=jnp.int32), 0, parts - 1)
    near = jnp.sum(
        jnp.where(
            around[None, :, None, None] == tile_ids[None, None, :, None], source[:, None], 0
        ),
        axis=2,
    )
    holder = jnp.sum(jnp.where(near[..., None] == tile_ids, owner_map, 0), axis=-1)
    second = jnp.any(
        jnp.logical_and(
            near[..., :, None] == near[..., None, :], number[None, :] < number[:, None]
        ),
        axis=-1,
    )
    places = (holder * 2 + second.astype(jnp.int32)).reshape(-1)

    banded_one, banded_two, gain, lift = pl.pallas_call(
        band_kernel,
        out_shape=(
            pltpu.VMEM((HID_ROWS * 8, 9 * WIN_ROWS), BF16),
            pltpu.VMEM((192, 240), BF16),
            pltpu.VMEM((8, 128), F32),
            pltpu.VMEM((64, 128), F32),
        ),
        in_specs=[smem(), smem(), vmem(), vmem()],
        out_specs=(vmem(),) * 4,
        name="bands",
    )(bias_one, bias_two, weight_one.reshape(8, 27), weight_two.reshape(8, 216))

    received, places, banded_one, banded_two, gain, lift = lax.optimization_barrier(
        (received, places, banded_one, banded_two, gain, lift)
    )
    image = pl.pallas_call(
        assemble_kernel,
        out_shape=pltpu.VMEM((sections, IMG_ROWS, W), BF16),
        in_specs=[smem(), vmem()],
        out_specs=vmem(),
        compiler_params=pltpu.CompilerParams(vmem_limit_bytes=32 << 20),
        name="assemble",
    )(in_smem(places), in_vmem(received))

    before = lax.ppermute(image, "gz", [(i, (i + 1) % depth) for i in range(depth)])
    after = lax.ppermute(image, "gz", [((i + 1) % depth, i) for i in range(depth)])

    return pl.pallas_call(
        conv_kernel,
        out_shape=jax.ShapeDtypeStruct((8, sections, 64, W), BF16),
        in_specs=[vmem()] * 7,
        out_specs=pl.BlockSpec(memory_space=pl.ANY),
        scratch_shapes=[
            pltpu.VMEM((6, 3, IMG_ROWS, W), F32),
            pltpu.VMEM((4, 66 * 8, W), BF16),
            pltpu.VMEM((8, sections, 64, W), BF16),
            pltpu.SemaphoreType.DMA((4 * sections,)),
        ],
        name="convolve",
    )(
        in_vmem(gain),
        in_vmem(lift),
        in_vmem(before),
        in_vmem(image),
        in_vmem(after),
        in_vmem(banded_one),
        in_vmem(banded_two),
    )


def solution(mesh):
    in_specs = (
        P("gz", "xy", None, None),
        P("gz", None, None),
        P("gz", None),
        P("gz", None),
        P("gz", None),
        P(),
        P(),
        P(),
        P(),
        P(),
    )
    out_specs = P(None, "gz", "xy", None)
    return jax.shard_map(
        on_device, mesh=mesh, in_specs=in_specs, out_specs=out_specs, check_vma=False
    )
```

```python
import jax
import jax.numpy as jnp
from jax import lax
from jax.experimental import pallas as pl
from jax.experimental.pallas import tpu as pltpu
from jax.sharding import PartitionSpec as P

SUB = 32
W = 512
HID_ROWS = 22
WIN_ROWS = 24
IMG_ROWS = 72
BATCH = 8
MAIN_UNROLL = 8
HALO_UNROLL = 4
F32 = jnp.float32
BF16 = jnp.bfloat16


def iota(shape, dim):
    return lax.broadcasted_iota(jnp.int32, shape, dim)


def by_index(which, choices):
    result = choices[-1]
    for number in range(len(choices) - 2, -1, -1):
        result = jnp.where(which == number, choices[number], result)
    return result


def step_right(block):
    first = iota((block.shape[0], 128), 1) == 0
    turned = [pltpu.roll(block[:, c : c + 128], 1, 1) for c in range(0, W, 128)]
    before = [0.0] + turned[:-1]
    return jnp.concatenate([jnp.where(first, x, y) for x, y in zip(before, turned)], axis=1)


def step_left(block):
    final = iota((block.shape[0], 128), 1) == 127
    turned = [pltpu.roll(block[:, c : c + 128], 127, 1) for c in range(0, W, 128)]
    after = turned[1:] + [0.0]
    return jnp.concatenate([jnp.where(final, x, y) for x, y in zip(after, turned)], axis=1)


def render_kernel(
    owner_in,
    source_in,
    tops_in,
    lefts_in,
    codes_in,
    tiles,
    out,
    owner,
    source,
    tops,
    lefts,
    codes,
    landing,
    wide,
    kept,
    ready,
    found,
    table,
    arrived,
    landed,
    listed,
    sent,
):
    parts = out.shape[0]
    sections = tiles.shape[0]
    small = [
        pltpu.make_async_copy(src, dst, arrived.at[n])
        for n, (src, dst) in enumerate(
            [
                (source_in, source),
                (owner_in, owner),
                (tops_in, tops),
                (lefts_in, lefts),
                (codes_in, codes),
            ]
        )
    ]
    half = landing.shape[1] // 2
    copies = [
        pltpu.make_async_copy(
            tiles.at[z, pl.ds(half * h, half), :],
            landing.at[z, pl.ds(half * h, half), :],
            landed.at[2 * z + h],
        )
        for z in range(sections)
        for h in range(2)
    ]
    for copy in small + copies:
        copy.start()
    count = source.shape[2]
    early, late = iota((128, 128), 0), iota((128, 128), 1)
    upto = jnp.logical_and(early // 32 == late // 32, early <= late).astype(F32).astype(BF16)
    strips = (iota((count, 128), 0) // 32 == iota((count, 128), 1)).astype(F32).astype(BF16)
    for copy in small[:2]:
        copy.wait()

    me = lax.axis_index("xy")
    mine = jnp.int32(0)
    for k in range(parts):
        mine = jnp.where(owner[k] == me, k, mine)
    blank = jnp.full((8 - sections, count), -1, jnp.int32)
    match = jnp.concatenate([source[z] for z in range(sections)] + [blank], axis=0) == mine
    marks = match.astype(F32)
    tall = jnp.concatenate([marks[:, t : t + 128] for t in range(0, count, 128)], axis=0)
    ranks = jnp.dot(tall.astype(BF16), upto, preferred_element_type=F32)
    rank = jnp.concatenate([ranks[t : t + 8] for t in range(0, count // 16, 8)], axis=1)
    for copy in small[2:]:
        copy.wait()
    packed = tops[...] + (lefts[...] << 9) + (codes[...] << 18)
    packed = jnp.concatenate([packed, blank], axis=0)
    pieces = []
    for slot in range(2):
        chosen = jnp.where(jnp.logical_and(match, rank == slot + 1), packed, 0)
        for k in range(3):
            pieces.append(((chosen >> (8 * k)) & 255).astype(F32))
    sums = jnp.dot(
        jnp.concatenate(pieces, axis=0).astype(BF16), strips, preferred_element_type=F32
    ).astype(jnp.int32)
    pair = [
        sums[24 * slot : 24 * slot + 8]
        + (sums[24 * slot + 8 : 24 * slot + 16] << 8)
        + (sums[24 * slot + 16 : 24 * slot + 24] << 16)
        for slot in range(2)
    ]
    merged = jnp.where(iota((8, 128), 0) < 2, pair[0], pltpu.roll(pair[1], 2, 0))
    found[...] = merged[0:4]
    listing = pltpu.make_async_copy(found, table, listed.at[0])
    listing.start()

    for z in range(sections):
        for h in range(2):
            copies[2 * z + h].wait()
            rows = pl.ds(half * h, half)
            for t in range(4):
                wide[z, t, rows, :] = landing[z, rows, 128 * t : 128 * t + 128].astype(F32)
    listing.wait()
    lane = iota((8, 128), 1)
    group = lane // 32
    starts = lane % 32 == 0

    def one(q, z, slot):
        code = table[2 * slot + z, q]
        y = code & 511
        x = (code >> 9) & 511
        a = ((code >> 20) & 3).astype(F32) * 0.25
        b = ((code >> 18) & 3).astype(F32) * 0.25
        near = x >> 7
        far = jnp.minimum(near + 1, 3)
        low = x & 127
        wraps = lane < low
        here = []
        for g in range(4):
            upper = jnp.where(
                wraps, wide[z, far, pl.ds(y + 8 * g, 8), :], wide[z, near, pl.ds(y + 8 * g, 8), :]
            )
            lower = jnp.where(
                wraps,
                wide[z, far, pl.ds(y + (8 * g + 1), 8), :],
                wide[z, near, pl.ds(y + (8 * g + 1), 8), :],
            )
            mixed = (1.0 - a) * upper + a * lower
            here.append(mixed if g == 0 else pltpu.roll(mixed, 32 * g, 1))
        turn = (lane - low) & 127
        left = by_index(turn >> 5, here)
        spill = by_index(turn >> 5, here[3:] + here[:3])
        right = pltpu.roll(jnp.where((turn & 31) == 0, spill, left), 127, 1)
        value = (1.0 - b) * left + b * right
        zs = z * 2 + slot
        ready[q, zs] = pltpu.roll(value, (128 - low) & 127, 1).astype(BF16)
        kept[q, zs] = pltpu.roll(value, (32 * zs + 128 - low) & 127, 1)

    sub = iota((8, 128), 0)
    which = jnp.where(sub < 4, group, (group + 1) & 3)

    def finish(batch):
        @pl.loop(0, BATCH, unroll=HALO_UNROLL)
        def _(step):
            q = batch * BATCH + step
            after = jnp.minimum(q + 1, parts - 1)
            before = jnp.maximum(q - 1, 0)
            both = [
                jnp.where(sub < 4, kept[after, zs], kept[before, zs]) for zs in range(2 * sections)
            ]
            ready[q, 2 * sections] = by_index(which, both).astype(BF16)

        sending(batch).start()

    def sending(batch):
        strips = pl.ds(batch * BATCH, BATCH)
        return pltpu.make_async_copy(ready.at[strips], out.at[strips], sent.at[batch])

    batches = parts // BATCH

    @pl.loop(0, batches)
    def _(batch):
        @pl.loop(0, BATCH, unroll=MAIN_UNROLL)
        def _(step):
            for z in range(sections):
                for slot in range(2):
                    one(batch * BATCH + step, z, slot)

        @pl.when(batch > 0)
        def _():
            finish(batch - 1)

    finish(batches - 1)

    @pl.loop(0, batches)
    def _(batch):
        sending(batch).wait()


def assemble_kernel(table, pool, image):
    me = lax.axis_index("xy")
    bottom = lax.axis_size("xy") - 1
    lane = iota((8, 128), 1)
    group = lane // 32
    sections = image.shape[0]

    def entry(z, strip, s):
        packed = table[(z * 3 + strip) * 32 + s]
        return packed >> 1, 2 * z + (packed & 1)

    for z in range(sections):
        for c in range(4):
            rows = []
            heads, feet = [], []
            for v in range(4):
                k, zs = entry(z, 0, 16 + 4 * c + v)
                piece = pool[k, 4].astype(F32)
                heads.append(pltpu.roll(piece, (32 * (v - zs - 3) + 256) & 127, 1))
                k, zs = entry(z, 2, 4 * c + v)
                piece = pool[k, 4].astype(F32)
                feet.append(pltpu.roll(piece, (32 * (v - zs) + 256) & 127, 1))
            rows.append(jnp.where(me == 0, 0.0, by_index(group, heads)))
            for u in range(2):
                blocks = []
                for v in range(4):
                    k, zs = entry(z, 1, 16 * u + 4 * c + v)
                    blocks.append(pool[k, zs].astype(F32))
                for g in range(4):
                    turned = [
                        blocks[v] if v == g else pltpu.roll(blocks[v], (32 * (v - g)) % 128, 1)
                        for v in range(4)
                    ]
                    rows.append(by_index(group, turned))
            rows.append(jnp.where(me == bottom, 0.0, by_index(group, feet)))
            strip = jnp.concatenate(rows, axis=0)[4:76]
            image[z, :, 128 * c : 128 * c + 128] = strip.astype(BF16)


def band_kernel(bias_one, bias_two, flat_one, flat_two, one, two, gain, lift):
    row = iota(gain.shape, 0)
    gain[...] = by_index(row, [bias_one[o] for o in range(8)])
    row = iota(lift.shape, 0) // 8
    lift[...] = by_index(row, [bias_two[o] for o in range(8)])
    rows, cols = one.shape
    col = iota((27, cols), 1)
    base = (col // WIN_ROWS) % 3 * 9 + col // (3 * WIN_ROWS)
    offset = iota((rows, cols), 1) % WIN_ROWS - iota((rows, cols), 0) // 8
    total = jnp.zeros((rows, cols), F32)
    for e in range(3):
        picks = (iota((27, cols), 0) == base + 3 * e).astype(F32).astype(BF16)
        taps = jnp.dot(flat_one[...], picks, preferred_element_type=F32)
        total = jnp.where(offset == e, jnp.concatenate([taps] * (rows // 8), axis=0), total)
    one[...] = total.astype(BF16)

    rows, cols = two.shape
    col = iota((216, cols), 1)
    base = col % 8 * 27 + col // 80 * 9
    spread = (iota((rows, 24), 0) // 8 == iota((rows, 24), 1)).astype(F32).astype(BF16)
    offset = iota((rows, cols), 1) % 80 // 8 - iota((rows, cols), 0) % 8
    total = jnp.zeros((rows, cols), F32)
    for e in range(3):
        parts = []
        for f in range(3):
            picks = (iota((216, cols), 0) == base + (3 * e + f)).astype(F32).astype(BF16)
            parts.append(jnp.dot(flat_two[...], picks, preferred_element_type=F32))
        taps = jnp.concatenate(parts, axis=0).astype(BF16)
        total = jnp.where(offset == e, jnp.dot(spread, taps, preferred_element_type=F32), total)
    two[...] = total.astype(BF16)


def conv_kernel(
    gain_in, lift_in, before, own, after, one, two, out, shifted, hidden, stage, sent
):
    me, deep = lax.axis_index("xy"), lax.axis_index("gz")
    bottom, last = lax.axis_size("xy") - 1, lax.axis_size("gz") - 1
    for number, (ref, z) in enumerate(
        [(before, 0), (before, 1), (own, 0), (own, 1), (after, 0), (after, 1)]
    ):
        plane = ref[z].astype(F32)
        if number < 2:
            plane = jnp.where(deep == 0, 0.0, plane)
        if number >= 4:
            plane = jnp.where(deep == last, 0.0, plane)
        shifted[number, 0] = step_right(plane)
        shifted[number, 1] = plane
        shifted[number, 2] = step_left(plane)
    gain = jnp.concatenate([gain_in[...]] * 4, axis=1)
    lift = jnp.concatenate([lift_in[...]] * 4, axis=1)
    height = HID_ROWS * 8

    weights, biases = [one[...]] * 4, [gain] * 4
    weights[0], biases[0] = jnp.where(deep > 0, one[...], 0), jnp.where(deep > 0, gain, 0.0)
    weights[3], biases[3] = jnp.where(deep < last, one[...], 0), jnp.where(deep < last, gain, 0.0)

    def first_layer(p, b):
        start = HID_ROWS * b + 2
        stack = jnp.concatenate(
            [
                shifted[p + d, f, start : start + WIN_ROWS, :]
                for f in range(3)
                for d in range(3)
            ],
            axis=0,
        ).astype(BF16)
        total = jnp.dot(weights[p], stack, preferred_element_type=F32)
        total = jnp.maximum(total.reshape(HID_ROWS, 8, W) + biases[p], 0.0)
        layers = [total[r] for r in range(HID_ROWS)]
        if b == 0:
            layers[0] = jnp.where(me > 0, layers[0], 0.0)
        if b == 2:
            layers[-1] = jnp.where(me < bottom, layers[-1], 0.0)
        total = jnp.concatenate(layers, axis=0)
        hidden[p, height * b : height * b + height, :] = total.astype(BF16)

    def second_layer(z, pair):
        halves = []
        for b in (2 * pair, 2 * pair + 1):
            stack = jnp.concatenate(
                [hidden[z + d, 64 * b : 64 * b + 80, :] for d in range(3)], axis=0
            )
            total = jnp.dot(two[...], stack, preferred_element_type=F32)
            left, right = step_right(total[0:64]), step_left(total[128:192])
            halves.append(total[64:128] + left + right + lift)
        rows = pl.ds(16 * pair, 16)
        for o in range(8):
            both = jnp.concatenate([half[8 * o : 8 * o + 8] for half in halves], axis=0)
            stage[o, z, rows, :] = both.astype(BF16)
        copy = pltpu.make_async_copy(
            stage.at[:, z, rows, :], out.at[:, z, rows, :], sent.at[4 * z + pair]
        )
        copy.start()
        return copy

    copies = []
    for p in range(4):
        first_layer(p, 0)
    for b, pairs in enumerate(((0,), (1,), (2, 3))):
        if b < 2:
            for p in range(4):
                first_layer(p, b + 1)
        copies += [second_layer(z, pair) for pair in pairs for z in range(2)]
    for copy in copies:
        copy.wait()


def smem():
    return pl.BlockSpec(memory_space=pltpu.SMEM)


def vmem():
    return pl.BlockSpec(memory_space=pltpu.VMEM)


def in_vmem(array):
    return pltpu.with_memory_space_constraint(array, pltpu.VMEM)


def in_smem(array):
    return pltpu.with_memory_space_constraint(array, pltpu.SMEM)


def on_device(
    raw_tiles,
    src_tile,
    shift_y,
    shift_x,
    subpixel,
    owner_map,
    weight_one,
    bias_one,
    weight_two,
    bias_two,
):
    parts = lax.axis_size("xy")
    depth = lax.axis_size("gz")
    me = lax.axis_index("xy")
    deep = lax.axis_index("gz")
    sections = raw_tiles.shape[0]
    source = src_tile.reshape(sections, parts, 32)
    tile_ids = jnp.arange(parts, dtype=jnp.int32)
    number = jnp.arange(32, dtype=jnp.int32)

    outgoing = pl.pallas_call(
        render_kernel,
        out_shape=jax.ShapeDtypeStruct((parts, 5, 8, 128), BF16),
        in_specs=[pl.BlockSpec(memory_space=pl.ANY)] * 6,
        out_specs=pl.BlockSpec(memory_space=pl.ANY),
        scratch_shapes=[
            pltpu.SMEM((parts,), jnp.int32),
            pltpu.VMEM((sections, 1, parts * 32), jnp.int32),
            pltpu.VMEM((sections, parts * 32), jnp.int32),
            pltpu.VMEM((sections, parts * 32), jnp.int32),
            pltpu.VMEM((sections, parts * 32), jnp.int32),
            pltpu.VMEM((sections, 512, 512), BF16),
            pltpu.VMEM((sections, 4, 512, 128), F32),
            pltpu.VMEM((parts, 2 * sections, 8, 128), F32),
            pltpu.VMEM((parts, 5, 8, 128), BF16),
            pltpu.VMEM((2 * sections, 128), jnp.int32),
            pltpu.SMEM((2 * sections, 128), jnp.int32),
            pltpu.SemaphoreType.DMA((5,)),
            pltpu.SemaphoreType.DMA((2 * sections,)),
            pltpu.SemaphoreType.DMA((1,)),
            pltpu.SemaphoreType.DMA((parts // BATCH,)),
        ],
        name="render",
    )(
        owner_map,
        src_tile.reshape(sections, 1, parts * 32),
        shift_y,
        shift_x,
        subpixel,
        raw_tiles.reshape(sections, 512, 512),
    )

    received = lax.all_to_all(outgoing, "xy", split_axis=0, concat_axis=0, tiled=True)

    around = jnp.clip(me + jnp.arange(-1, 2, dtype=jnp.int32), 0, parts - 1)
    near = jnp.sum(
        jnp.where(
            around[None, :, None, None] == tile_ids[None, None, :, None], source[:, None], 0
        ),
        axis=2,
    )
    holder = jnp.sum(jnp.where(near[..., None] == tile_ids, owner_map, 0), axis=-1)
    second = jnp.any(
        jnp.logical_and(
            near[..., :, None] == near[..., None, :], number[None, :] < number[:, None]
        ),
        axis=-1,
    )
    places = (holder * 2 + second.astype(jnp.int32)).reshape(-1)

    banded_one, banded_two, gain, lift = pl.pallas_call(
        band_kernel,
        out_shape=(
            pltpu.VMEM((HID_ROWS * 8, 9 * WIN_ROWS), BF16),
            pltpu.VMEM((192, 240), BF16),
            pltpu.VMEM((8, 128), F32),
            pltpu.VMEM((64, 128), F32),
        ),
        in_specs=[smem(), smem(), vmem(), vmem()],
        out_specs=(vmem(),) * 4,
        name="bands",
    )(bias_one, bias_two, weight_one.reshape(8, 27), weight_two.reshape(8, 216))

    received, places, banded_one, banded_two, gain, lift = lax.optimization_barrier(
        (received, places, banded_one, banded_two, gain, lift)
    )
    image = pl.pallas_call(
        assemble_kernel,
        out_shape=pltpu.VMEM((sections, IMG_ROWS, W), BF16),
        in_specs=[smem(), vmem()],
        out_specs=vmem(),
        compiler_params=pltpu.CompilerParams(vmem_limit_bytes=32 << 20),
        name="assemble",
    )(in_smem(places), in_vmem(received))

    before = lax.ppermute(image, "gz", [(i, (i + 1) % depth) for i in range(depth)])
    after = lax.ppermute(image, "gz", [((i + 1) % depth, i) for i in range(depth)])

    return pl.pallas_call(
        conv_kernel,
        out_shape=jax.ShapeDtypeStruct((8, sections, 64, W), BF16),
        in_specs=[vmem()] * 7,
        out_specs=pl.BlockSpec(memory_space=pl.ANY),
        scratch_shapes=[
            pltpu.VMEM((6, 3, IMG_ROWS, W), F32),
            pltpu.VMEM((4, 66 * 8, W), BF16),
            pltpu.VMEM((8, sections, 64, W), BF16),
            pltpu.SemaphoreType.DMA((4 * sections,)),
        ],
        name="convolve",
    )(
        in_vmem(gain),
        in_vmem(lift),
        in_vmem(before),
        in_vmem(image),
        in_vmem(after),
        in_vmem(banded_one),
        in_vmem(banded_two),
    )


def solution(mesh):
    in_specs = (
        P("gz", "xy", None, None),
        P("gz", None, None),
        P("gz", None),
        P("gz", None),
        P("gz", None),
        P(),
        P(),
        P(),
        P(),
        P(),
    )
    out_specs = P(None, "gz", "xy", None)
    return jax.shard_map(
        on_device, mesh=mesh, in_specs=in_specs, out_specs=out_specs, check_vma=False
    )
```
